256 devices in a mesh: area: 32 (over x, z), col: 8 (over y, core).
Axes of the slice: x: 4, y: 4, z: 8, core: 2. Of those that a mesh axis runs over, the one named last changes fastest.
Arguments:
- initial_state: float32 [2048, 128, 128], P(('area', 'col')), may hold values from -6 to 6
- past_rates: bfloat16 [2, 2048, 128, 128], P(None, ('area', 'col')), may hold values from 0 to 2
- stimulus: bfloat16 [2048, 128, 128], P(('area', 'col')), may hold values from -6 to 6
- leak_rate: float32 [2048, 128], P(('area', 'col')), may hold values from 0.05 to 0.5
- local_weight: bfloat16 [2048, 12, 128, 128], P(('area', 'col')), may hold values from -0.125 to 0.125
- far_weight: bfloat16 [2048, 8, 128, 128], P(('area', 'col')), may hold values from -0.125 to 0.125
- local_index: int32 [2048, 12], P(('area', 'col')), may hold values from 0 to 63, all different within a row
- area_sizes: int32 [8], replicated, may hold values from 1 to 12, as said below
- far_area: int32 [2048, 8], replicated, may hold values from 0 to 7, as said below
- far_offset: int32 [2048, 8], replicated, may hold values from 0 to 767, as said below
Outputs:
- final_state: float32 [2048, 128, 128], P(('area', 'col'))
The draws below stay inside these ranges and needn't reach their ends.
Inputs may be any that keep to these rules, and one draw needn't show every extreme that they name: `area_sizes`: Areas' section counts sum to 32; some area has exactly 12 sections. `far_area`: the source area of a far link differs from the area that holds its block row. In each aligned group of 8 block rows, at most 4 far links read blocks of one section (blocks s * 64 to s * 64 + 63), and exactly 4 read some section. `far_offset`: each offset lies below its source area's sections times 64.
All inputs are finite; a program needn't handle non-finite values.
Results may differ from the reference program's by a relative error of at most 0.0009.
Values may be sent and summed in bfloat16 or wider, within the bound.
No kernel may reach another device: no remote copies, remote signals or barrier semaphores. Data moves between devices by JAX's collectives and lax.ppermute only.
A program may use at most 128 MiB of HBM per device.

```python
import math
import jax
import jax.numpy as jnp
from jax import lax

BLOCK = 128
TRIALS = 128
BLK_DEV = 8
LOCAL = 12
FAR = 8
AREAS = 8
STEPS = 4
DELAY = 2
SEC_BLK = 64
NB = 2048
MOST_AREA = 12
CAP = 4
N_AREA = 32
N_COL = 8


def link_tables(key):
    base = jax.random.fold_in(key, 7)
    key_big, key_spread, key_device = jax.random.split(base, 3)
    extra_cap = max(MOST_AREA - 1, 1)
    big_area = jax.random.randint(key_big, (), 0, AREAS)
    slot_area = jnp.arange(AREAS * extra_cap, dtype=jnp.int32) // extra_cap
    priority = jax.random.permutation(key_spread, AREAS * extra_cap).astype(jnp.int32)
    priority = jnp.where(slot_area == big_area, AREAS * extra_cap + priority, priority)
    slot_rank = jnp.argsort(jnp.argsort(priority))
    spread_total = N_AREA - AREAS - (MOST_AREA - 1)
    chosen = (slot_rank < spread_total).astype(jnp.int32)
    area_ids = jnp.arange(AREAS, dtype=jnp.int32)
    counts = jnp.sum(chosen[None, :] * (slot_area[None, :] == area_ids[:, None]).astype(jnp.int32), axis=1)
    sizes = (1 + counts + (MOST_AREA - 1) * (area_ids == big_area).astype(jnp.int32)).astype(jnp.int32)
    starts = jnp.cumsum(sizes) - sizes
    section_ids = jnp.arange(N_AREA, dtype=jnp.int32)
    area_of_section = (jnp.sum((starts[None, :] <= section_ids[:, None]).astype(jnp.int32), axis=1) - 1).astype(jnp.int32)
    device_count = N_AREA * N_COL
    link_count = BLK_DEV * FAR
    device_ids = jnp.arange(device_count, dtype=jnp.int32)
    own_area = area_of_section[device_ids // N_COL]

    def one_device(device_key, home_area):
        key_forced, key_order, key_shuffle, key_within = jax.random.split(device_key, 4)
        slot_section = jnp.arange(N_AREA * CAP, dtype=jnp.int32) // CAP
        eligible = area_of_section[slot_section] != home_area
        section_ok = area_of_section != home_area
        scores = jax.random.randint(key_forced, (N_AREA,), 0, 1 << 20) * N_AREA + section_ids
        forced = jnp.argmax(jnp.where(section_ok, scores, -1))
        order_perm = jax.random.permutation(key_order, N_AREA * CAP).astype(jnp.int32)
        ranking = jnp.where(slot_section == forced, order_perm - 2 * N_AREA * CAP, order_perm)
        ranking = jnp.where(eligible, ranking, order_perm + 2 * N_AREA * CAP)
        picked = jnp.argsort(ranking)[:link_count]
        shuffle = jax.random.permutation(key_shuffle, link_count)
        slots = picked[shuffle]
        section_pick = (slots // CAP).astype(jnp.int32)
        within = jax.random.randint(key_within, (link_count,), 0, SEC_BLK)
        return (section_pick, within)
    device_keys = jax.vmap(lambda number: jax.random.fold_in(key_device, number))(device_ids)
    section_pick, within = jax.vmap(one_device)(device_keys, own_area)
    source_area = area_of_section[section_pick]
    offsets = (section_pick - starts[source_area]) * SEC_BLK + within
    return (sizes, source_area.reshape(NB, FAR).astype(jnp.int32), offsets.reshape(NB, FAR).astype(jnp.int32))


def draw_area_sizes(key, part):
    return link_tables(key)[0]


def draw_far_area(key, part):
    return link_tables(key)[1]


def draw_far_offset(key, part):
    return link_tables(key)[2]


def shard_levels(stream_key, dims, cuts, smallest, high):
    level, own = 1.0, jax.random.fold_in(stream_key, 6)
    for dim, shards_of in cuts:
        heights = jnp.exp(jax.random.uniform(jax.random.fold_in(own, dim), (shards_of,), jnp.float32, smallest / len(cuts), high / len(cuts)))
        level = level * jnp.repeat(heights, dims[dim] // shards_of).reshape([-1 if axis == dim else 1 for axis in range(len(dims))])
    return level


def distinct(stream_key, rows, amount, top, lift):
    sequence = jax.random.permutation(jax.random.fold_in(stream_key, 1), amount)
    boost = sequence
    for power in range(3):
        boost = boost * boost // amount
    boost = boost * lift // amount
    tickets = jax.random.randint(jax.random.fold_in(stream_key, 2), (rows, amount), 0, 4096) + boost
    holders = jax.random.permutation(jax.random.fold_in(stream_key, 3), rows)[jnp.arange(amount) % rows]
    tickets = jnp.where(jnp.arange(rows)[:, None] == holders[None, :], 1 << 14, tickets)
    merit = tickets * amount + jnp.arange(amount)
    return lax.top_k(merit.astype(jnp.int32), top)[1].astype(jnp.int32)


def scatter_about(stream_key, dims, deviation, most, cuts=(), kind=jnp.bfloat16):
    entries = jax.random.normal(stream_key, dims, jnp.float32) * deviation
    if len(cuts) > 0:
        entries = shard_levels(stream_key, dims, cuts, -0.22, 0.18) * entries
    return jnp.clip(entries, min=-most, max=most).astype(kind)


def setup_inputs(seed: int = 0) -> dict:
    streams_of = jax.random.split(jax.random.key(seed), 11)
    initial_state = scatter_about(streams_of[0], (NB, TRIALS, BLOCK), 1.0, 6.0, ((0, 256),), jnp.float32)
    past_rates = jnp.clip(2.0 * jax.random.uniform(streams_of[1], (DELAY, NB, TRIALS, BLOCK), jnp.float32) ** shard_levels(streams_of[1], (DELAY, NB, TRIALS, BLOCK), ((1, 256),), -0.2, 0.2), 0.0, 2.0).astype(jnp.bfloat16)
    stimulus = scatter_about(streams_of[2], (NB, TRIALS, BLOCK), 1.0, 6.0, ((0, 256),))
    leak_rate = jnp.clip(jnp.exp(math.log(0.5) - 2.3025851 * jax.random.uniform(streams_of[3], (NB, BLOCK), jnp.float32) ** shard_levels(streams_of[3], (NB, BLOCK), ((0, 256),), -0.2, 0.2)), 0.05, 0.5)
    local_weight = scatter_about(streams_of[4], (NB, LOCAL, BLOCK, BLOCK), ((LOCAL + FAR) * BLOCK) ** -0.5, 0.125, ((0, 256),))
    far_weight = scatter_about(streams_of[5], (NB, FAR, BLOCK, BLOCK), ((LOCAL + FAR) * BLOCK) ** -0.5, 0.125, ((0, 256),))
    local_index = distinct(streams_of[6], NB, SEC_BLK, LOCAL, 3072)
    area_sizes = draw_area_sizes(jax.random.fold_in(streams_of[10], 71), 0)
    far_area = draw_far_area(jax.random.fold_in(streams_of[10], 71), 0)
    far_offset = draw_far_offset(jax.random.fold_in(streams_of[10], 71), 0)
    return dict(initial_state=initial_state, past_rates=past_rates, stimulus=stimulus, leak_rate=leak_rate, local_weight=local_weight, far_weight=far_weight, local_index=local_index, area_sizes=area_sizes, far_area=far_area, far_offset=far_offset)


def reference(initial_state, past_rates, stimulus, leak_rate, local_weight, far_weight, local_index, area_sizes, far_area, far_offset):
    area_first = (jnp.cumsum(area_sizes) - area_sizes).astype(jnp.int32)
    area_len = area_sizes[far_area].astype(jnp.int32)
    first_sel = area_first[far_area].astype(jnp.int32)
    far_block = (first_sel * SEC_BLK + far_offset % (area_len * SEC_BLK)).astype(jnp.int32)
    row_ids = jnp.arange(NB, dtype=jnp.int32)
    local_block = (((row_ids // SEC_BLK) * SEC_BLK)[:, None] + local_index).astype(jnp.int32)

    def currents(rate_now, rate_late):
        def per_group(inputs):
            near_ids, far_ids, near_weight, distant_weight = inputs
            lateral = jnp.einsum("rktb,rkob->rto", rate_now[near_ids].astype(jnp.float32), near_weight.astype(jnp.float32), precision=lax.Precision.HIGHEST)
            distant = jnp.einsum("rktb,rkob->rto", rate_late[far_ids].astype(jnp.float32), distant_weight.astype(jnp.float32), precision=lax.Precision.HIGHEST)
            return lateral, distant

        lateral, distant = lax.map(per_group, (
            local_block.reshape(N_AREA, SEC_BLK, LOCAL),
            far_block.reshape(N_AREA, SEC_BLK, FAR),
            local_weight.reshape(N_AREA, SEC_BLK, LOCAL, BLOCK, BLOCK),
            far_weight.reshape(N_AREA, SEC_BLK, FAR, BLOCK, BLOCK)))
        return lateral.reshape(NB, TRIALS, BLOCK), distant.reshape(NB, TRIALS, BLOCK)

    membrane = initial_state
    history = [past_rates[index] for index in range(DELAY)]
    history.append(jax.nn.softplus(membrane).astype(jnp.bfloat16))
    drive_term = stimulus.astype(jnp.float32)
    for step_idx in range(STEPS):
        lateral, distant = currents(history[step_idx + DELAY], history[step_idx])
        membrane = membrane + leak_rate[:, None, :] * (-membrane + lateral + distant + drive_term)
        if step_idx + 1 < STEPS:
            history.append(jax.nn.softplus(membrane).astype(jnp.bfloat16))
    return membrane
```

```python
import jax
import jax.numpy as jnp
from jax import lax
from jax.experimental import pallas as pl
from jax.experimental.pallas import tpu as pltpu
from jax.sharding import Mesh, PartitionSpec as P

STEPS = 4
NX, NZ, NY, NC = 4, 8, 4, 2
ROWS = 8
LOCAL = 12
FAR = 8
LINKS = ROWS * FAR
BLK = 128
SEC = 64
CAP = 32
GROUPS = 2 * NX
LIST = GROUPS * CAP
UNROLL = 8
NA = 5
NB = ROWS - NA
PIECES = 18
F32 = jnp.float32
BF16 = jnp.bfloat16
FETCH = LIST
STARTS = 2 * LIST
BOUNDS = STARTS + GROUPS + 1


def ring(n, shift):
    return [(i, (i + shift) % n) for i in range(n)]


def shift(a, axis, by):
    return lax.ppermute(a, axis, ring({"x": NX, "y": NY, "z": NZ}[axis], by))


def swap(a):
    return lax.ppermute(a, "c", [(0, 1), (1, 0)])


def any_spec():
    return pl.BlockSpec(memory_space=pl.ANY)


def vmem_spec():
    return pl.BlockSpec(memory_space=pltpu.VMEM)


def smem_spec():
    return pl.BlockSpec(memory_space=pltpu.SMEM)


def pack_kernel(meta_ref, *refs):
    pieces, out_ref = refs[:GROUPS], refs[GROUPS]
    held, sem, out_sem = refs[GROUPS + 1 :]
    for q, piece in enumerate(pieces):

        def start(p, carry, piece=piece):
            rank = (meta_ref[p] >> 6) & 31
            pltpu.make_async_copy(piece.at[rank], held.at[p], sem).start()
            return carry

        lax.fori_loop(meta_ref[STARTS + q], meta_ref[STARTS + q + 1], start, 0)

    def wait(p, carry):
        pltpu.make_async_copy(pieces[0].at[0], held.at[0], sem).wait()
        return carry

    count = meta_ref[STARTS + GROUPS]
    lax.fori_loop(0, count, wait, 0)

    def out_copy(i):
        span = pl.ds(pl.multiple_of(i * UNROLL, UNROLL), UNROLL)
        return pltpu.make_async_copy(held.at[span], out_ref.at[span], out_sem)

    def start_out(i, carry):
        out_copy(i).start()
        return carry

    def wait_out(i, carry):
        out_copy(i).wait()
        return carry

    chunks = (count + UNROLL - 1) // UNROLL
    lax.fori_loop(0, chunks, start_out, 0)
    lax.fori_loop(0, chunks, wait_out, 0)


def pack_weights(meta, pieces):
    return pl.pallas_call(
        pack_kernel,
        out_shape=jax.ShapeDtypeStruct((LIST, BLK, BLK), BF16),
        in_specs=[smem_spec()] + [any_spec()] * GROUPS,
        out_specs=any_spec(),
        scratch_shapes=[
            pltpu.VMEM((LIST, BLK, BLK), BF16),
            pltpu.SemaphoreType.DMA,
            pltpu.SemaphoreType.DMA,
        ],
        name="pack_weights",
    )(meta, *pieces)


def make_partial_kernel(n_pieces, offset):
    def kernel(meta_ref, weight_ref, *refs):
        pieces = refs[:n_pieces]
        outs = refs[n_pieces : n_pieces + NX + 1]
        rates, weights, acc, rate_sem, weight_sem, out_sem = refs[n_pieces + NX + 1 :]
        count = meta_ref[STARTS + GROUPS]
        chunks = (count + UNROLL - 1) // UNROLL

        def weight_copy(i):
            span = pl.ds(pl.multiple_of(i * UNROLL, UNROLL), UNROLL)
            return pltpu.make_async_copy(weight_ref.at[span], weights.at[span], weight_sem)

        def start_weight(i, carry):
            weight_copy(i).start()
            return carry

        lax.fori_loop(0, chunks, start_weight, 0)
        if n_pieces == 1:

            def start_rate(p, carry):
                place = (meta_ref[p] >> 11) & 511
                pltpu.make_async_copy(
                    pieces[0].at[place + offset], rates.at[p], rate_sem
                ).start()
                return carry

            lax.fori_loop(0, count, start_rate, 0)
        else:
            for q, piece in enumerate(pieces):

                def start_rate(i, carry, piece=piece):
                    v = meta_ref[FETCH + i]
                    pltpu.make_async_copy(
                        piece.at[(v >> 8) & 63], rates.at[v & 255], rate_sem
                    ).start()
                    return carry

                lax.fori_loop(meta_ref[BOUNDS + q], meta_ref[BOUNDS + q + 1], start_rate, 0)
        acc[...] = jnp.zeros_like(acc)

        def wait_rate(p, carry):
            pltpu.make_async_copy(pieces[0].at[0], rates.at[0], rate_sem).wait()
            return carry

        def wait_weight(i, carry):
            weight_copy(i).wait()
            return carry

        lax.fori_loop(0, count, wait_rate, 0)
        lax.fori_loop(0, chunks, wait_weight, 0)

        def chunk(i, carry):
            prods = []
            for u in range(UNROLL):
                p = i * UNROLL + u
                row = jnp.where(p < count, meta_ref[p] & 63, GROUPS * ROWS)
                prod = lax.dot_general(
                    rates[p], weights[p], (((1,), (1,)), ((), ())), preferred_element_type=F32
                )
                prods.append((row, prod))
            for row, prod in prods:
                acc[row] += prod
            return carry

        lax.fori_loop(0, chunks, chunk, 0)
        copies = [
            pltpu.make_async_copy(acc.at[pl.ds(g * ROWS, ROWS)], outs[g], out_sem.at[g])
            for g in range(NX)
        ] + [
            pltpu.make_async_copy(
                acc.at[pl.ds(NX * ROWS, NX * ROWS)], outs[NX], out_sem.at[NX]
            )
        ]
        for copy in copies:
            copy.start()
        for copy in copies:
            copy.wait()

    return kernel


def partial_sums(meta, weights, pieces, offset):
    return pl.pallas_call(
        make_partial_kernel(len(pieces), offset),
        out_shape=[jax.ShapeDtypeStruct((ROWS, BLK, BLK), F32)] * NX
        + [jax.ShapeDtypeStruct((NX * ROWS, BLK, BLK), F32)],
        in_specs=[smem_spec()] + [any_spec()] * (1 + len(pieces)),
        out_specs=[any_spec()] * (NX + 1),
        scratch_shapes=[
            pltpu.VMEM((LIST, BLK, BLK), BF16),
            pltpu.VMEM((LIST, BLK, BLK), BF16),
            pltpu.VMEM((GROUPS * ROWS + 1, BLK, BLK), F32),
            pltpu.SemaphoreType.DMA,
            pltpu.SemaphoreType.DMA,
            pltpu.SemaphoreType.DMA((NX + 1,)),
        ],
        compiler_params=pltpu.CompilerParams(vmem_limit_bytes=40 * 1024 * 1024),
        name="partial_sums",
    )(meta, weights, *pieces)


def step_kernel(
    pos_ref,
    membrane_ref,
    stimulus_ref,
    leak_ref,
    weight_ref,
    f0_ref,
    f1_ref,
    f2_ref,
    f3_ref,
    *refs,
):
    pieces = refs[:GROUPS]
    out_ref, rate_ref = refs[GROUPS : GROUPS + 2]
    section, sems = refs[GROUPS + 2 :]
    copies = [
        pltpu.make_async_copy(piece, section.at[pl.ds(q * ROWS, ROWS)], sems.at[q])
        for q, piece in enumerate(pieces)
    ]
    for copy in copies:
        copy.start()
    for copy in copies:
        copy.wait()

    def row(i, carry):
        total = f0_ref[i] + f1_ref[i].astype(F32) + f2_ref[i].astype(F32) + f3_ref[i].astype(F32) + stimulus_ref[i].astype(F32)
        for k in range(0, LOCAL, 2):
            left = jnp.concatenate(
                [section[pos_ref[i * LOCAL + k]], section[pos_ref[i * LOCAL + k + 1]]], axis=1
            )
            right = jnp.concatenate([weight_ref[i, k], weight_ref[i, k + 1]], axis=1)
            total += lax.dot_general(
                left, right, (((1,), (1,)), ((), ())), preferred_element_type=F32
            )
        old = membrane_ref[i]
        new = old + leak_ref[pl.ds(i, 1), :] * (total - old)
        out_ref[i] = new
        soft = jnp.maximum(new, 0.0) + jnp.log1p(jnp.exp(-jnp.abs(new)))
        rate_ref[i] = soft.astype(BF16)
        return carry

    lax.fori_loop(0, ROWS, row, 0)


def step_of(pos, membrane, stimulus, leak, weights, far, pieces):
    return pl.pallas_call(
        step_kernel,
        out_shape=[
            jax.ShapeDtypeStruct((ROWS, BLK, BLK), F32),
            jax.ShapeDtypeStruct((ROWS, BLK, BLK), BF16),
        ],
        in_specs=[smem_spec()] + [vmem_spec()] * 8 + [any_spec()] * GROUPS,
        out_specs=[vmem_spec()] * 2,
        scratch_shapes=[
            pltpu.VMEM((SEC, BLK, BLK), BF16),
            pltpu.SemaphoreType.DMA((GROUPS,)),
        ],
        compiler_params=pltpu.CompilerParams(vmem_limit_bytes=24 * 1024 * 1024),
        name="step",
    )(pos, membrane, stimulus, leak, weights, *far, *pieces)


def after(value, *deps):
    return lax.optimization_barrier((value, *deps))[0]


def gather_plane(frame):
    a0, b0 = frame[:NA], frame[NA:]
    p1, p3, p2 = shift(b0, "y", 1), shift(b0, "y", -1), shift(b0, "y", 2)
    f1, g1 = shift(a0, "z", 1), shift(a0, "z", -1)
    first = jnp.concatenate([a0, f1, g1], axis=0)
    f2, g2 = shift(f1, "z", 1), shift(g1, "z", -1)
    f3, g3 = shift(f2, "z", 1), shift(g2, "z", -1)
    f4 = shift(f3, "z", 1)
    first, p1, p2, p3 = lax.optimization_barrier((first, p1, p2, p3))
    yb = jnp.concatenate([b0, p1, p2, p3], axis=0)
    u1, v1 = shift(first, "y", 1), shift(first, "y", -1)
    fs, gs = [yb], [yb]
    for _ in range(4):
        fs.append(shift(fs[-1], "z", 1))
    for _ in range(3):
        gs.append(shift(gs[-1], "z", -1))
    second = jnp.concatenate([f2, g2, f3, g3, f4], axis=0)
    second, u1, v1 = lax.optimization_barrier((second, u1, v1))
    u2, v2 = shift(second, "y", 1), shift(second, "y", -1)
    h1, h2 = (3 * NA + 1) // 2, (5 * NA + 1) // 2
    w11, w12 = shift(u1[:h1], "y", 1), shift(v1[h1:], "y", -1)
    w11, w12, u2, v2 = lax.optimization_barrier((w11, w12, u2, v2))
    w21, w22 = shift(u2[:h2], "y", 1), shift(v2[h2:], "y", -1)
    return [first, second, u1, u2, v1, v2, w11, w12, w21, w22, *fs, *gs[1:]]


EARLY, MIDDLE, LATE = 0, 1, 7


def lookup(index, table):
    return sum(jnp.where(index == i, v, 0) for i, v in enumerate(table))


def place_of(ez, ey, j):
    h1, h2 = (3 * NA + 1) // 2, (5 * NA + 1) // 2
    late = ((ez >= 2) & (ez <= 6)).astype(jnp.int32)
    off = lookup(ez, [0, 1, 0, 2, 4, 3, 1, 2]) * NA + j
    half = jnp.where(late == 1, h2, h1)
    upper = off >= half
    piece_a = jnp.where(
        ey == 2,
        6 + 2 * late + upper.astype(jnp.int32),
        lookup(ey, [0, 2, 0, 4]) + late,
    )
    off_a = jnp.where((ey == 2) & upper, off - half, off)
    piece_b = lookup(ez, [10, 11, 12, 13, 14, 17, 16, 15])
    off_b = ey * NB + j - NA
    in_a = j < NA
    return jnp.where(in_a, piece_a, piece_b), jnp.where(in_a, off_a, off_b)


def total_of(mask, axis=-1):
    return jnp.sum(mask, axis=axis, dtype=jnp.int32)


def shards(
    initial_state,
    past_rates,
    stimulus,
    leak_rate,
    local_weight,
    far_weight,
    local_index,
    area_sizes,
    far_area,
    far_offset,
):
    x, z, y, c = (lax.axis_index(n) for n in ("x", "z", "y", "c"))
    first_rate = jax.nn.softplus(initial_state).astype(BF16)
    plane0 = gather_plane(past_rates[0])
    both = lax.all_gather(
        jnp.concatenate([past_rates[1], first_rate], axis=0), ("z", "y"), axis=0, tiled=True
    )

    def mine(table):
        t = table.reshape(NX, NZ, NY, NC, LINKS)
        t = lax.dynamic_index_in_dim(t, z, 1, keepdims=False)
        return lax.dynamic_index_in_dim(t, y, 1, keepdims=False)

    area, offset = mine(far_area), mine(far_offset)
    ids = jnp.arange(area_sizes.shape[0], dtype=jnp.int32)
    starts = jnp.sum(jnp.where(ids[None, :] < ids[:, None], area_sizes[None, :], 0), axis=-1)
    match = area[..., None] == ids
    area_len = jnp.sum(jnp.where(match, area_sizes, 0), axis=-1)
    first = jnp.sum(jnp.where(match, starts, 0), axis=-1)
    block = first * SEC + offset % (area_len * SEC)
    plane = block >> 9
    lids = jnp.arange(LINKS, dtype=jnp.int32)
    earlier = lids[None, :] < lids[:, None]
    rank = total_of((plane[..., :, None] == plane[..., None, :]) & earlier)

    own = lambda t: lax.dynamic_index_in_dim(
        lax.dynamic_index_in_dim(t, x, 0, keepdims=False), c, 0, keepdims=False
    )
    own_plane, own_rank = own(plane), own(rank)
    hop = jnp.arange(NX, dtype=jnp.int32)
    slot = jnp.arange(CAP, dtype=jnp.int32)
    fits = (own_plane == ((x + hop) & 3)[:, None])[:, None, :] & (
        own_rank[None, None, :] == slot[None, :, None]
    )
    pick = after(jnp.sum(jnp.where(fits, lids, 0), axis=-1), plane0[EARLY])
    flat_weight = far_weight.reshape(LINKS, BLK, BLK)
    near = [flat_weight[pick[0]]] + [
        shift(flat_weight[pick[g]], "x", g) for g in range(1, NX)
    ]

    dest_x = jnp.arange(NX, dtype=jnp.int32)[:, None, None]
    dest_c = jnp.arange(NC, dtype=jnp.int32)[None, :, None]
    group = jnp.where(dest_c == c, 0, NX) + ((x - dest_x) & 3) + 0 * plane
    source_z, source_y, source_j = (block >> 6) & 7, (block >> 4) & 3, block & 7
    piece, off = place_of((z - source_z) & 7, (y - source_y) & 3, source_j)
    flat = lambda t: t.reshape(-1)
    works = flat((plane == x) & (((block >> 3) & 1) == c))
    order = flat(group * LINKS + lids)
    before = total_of(works[None, :] & (order[None, :] < order[:, None]))
    value = flat(
        group * ROWS + lids // FAR + (rank << 6) + ((source_z * 64 + source_y * 16 + source_j) << 11)
    )
    spots = jnp.arange(LIST, dtype=jnp.int32)
    links = jnp.sum(
        jnp.where(works[None, :] & (before[None, :] == spots[:, None]), value[None, :], 0), axis=-1
    )
    fetch_order = flat(piece) * 512 + order
    fetch_before = total_of(works[None, :] & (fetch_order[None, :] < fetch_order[:, None]))
    fetch_value = before + (flat(off) << 8)
    fetch = jnp.sum(
        jnp.where(
            works[None, :] & (fetch_before[None, :] == spots[:, None]), fetch_value[None, :], 0
        ),
        axis=-1,
    )
    group_starts = total_of(
        works[None, :] & (flat(group)[None, :] < jnp.arange(GROUPS + 1, dtype=jnp.int32)[:, None])
    )
    piece_starts = total_of(
        works[None, :] & (flat(piece)[None, :] < jnp.arange(PIECES + 1, dtype=jnp.int32)[:, None])
    )
    meta = jnp.concatenate([links, fetch, group_starts, piece_starts])
    weights = pack_weights(meta, near + [swap(w) for w in near])

    col = local_index >> 3
    local_pos = (
        jnp.where((col & 1) == c, 0, 32) + ((y - (col >> 1)) & 3) * 8 + (local_index & 7)
    ).reshape(-1)

    def far_input(pieces, offset):
        *kept, other = partial_sums(meta, weights, pieces, offset)
        other = swap(other).reshape(NX, ROWS, BLK, BLK)
        sums = [kept[g] + other[g] for g in range(NX)]
        return [sums[0]] + [shift(sums[g].astype(BF16), "x", -g) for g in range(1, NX)]

    def section_of(rate):
        parts = [rate] + [shift(rate, "y", g) for g in range(1, NY)]
        return parts + [swap(p) for p in parts]

    membrane, rate = initial_state, first_rate
    far = [far_input(plane0, 0), None, None, None]
    section = section_of(after(rate, plane0[MIDDLE]))
    for step in range(STEPS):
        if step > 0:
            section = section_of(rate)
        if step == 1:
            waited = after(both, rate)
            far[1], far[2] = far_input([waited], 0), far_input([waited], ROWS)
        membrane, rate = step_of(
            local_pos, membrane, stimulus, leak_rate, local_weight, far[step], section
        )
        if step == 0:
            plane3 = gather_plane(rate)
        if step == 1:
            plane3[LATE] = after(plane3[LATE], rate)
            far[3] = far_input(plane3, 0)
    return membrane


def solution(mesh):
    mesh4 = Mesh(mesh.devices.reshape(NX, NZ, NY, NC), ("x", "z", "y", "c"))
    dev = ("x", "z", "y", "c")
    return jax.shard_map(
        shards,
        mesh=mesh4,
        in_specs=(
            P(dev, None, None),
            P(None, dev, None, None),
            P(dev, None, None),
            P(dev, None),
            P(dev, None, None, None),
            P(dev, None, None, None),
            P(dev, None),
            P(),
            P(),
            P(),
        ),
        out_specs=P(dev, None, None),
        check_vma=False,
    )
```

```python
import jax
import jax.numpy as jnp
from jax import lax
from jax.experimental import pallas as pl
from jax.experimental.pallas import tpu as pltpu
from jax.sharding import Mesh, PartitionSpec as P

STEPS = 4
NX, NZ, NY, NC = 4, 8, 4, 2
ROWS = 8
LOCAL = 12
FAR = 8
LINKS = ROWS * FAR
BLK = 128
SEC = 64
CAP = 32
GROUPS = 2 * NX
LIST = GROUPS * CAP
UNROLL = 8
NA = 5
NB = ROWS - NA
PIECES = 18
F32 = jnp.float32
BF16 = jnp.bfloat16
FETCH = LIST
STARTS = 2 * LIST
BOUNDS = STARTS + GROUPS + 1


def ring(n, shift):
    return [(i, (i + shift) % n) for i in range(n)]


def shift(a, axis, by):
    return lax.ppermute(a, axis, ring({"x": NX, "y": NY, "z": NZ}[axis], by))


def swap(a):
    return lax.ppermute(a, "c", [(0, 1), (1, 0)])


def any_spec():
    return pl.BlockSpec(memory_space=pl.ANY)


def vmem_spec():
    return pl.BlockSpec(memory_space=pltpu.VMEM)


def smem_spec():
    return pl.BlockSpec(memory_space=pltpu.SMEM)


def pack_kernel(meta_ref, *refs):
    pieces, out_ref = refs[:GROUPS], refs[GROUPS]
    held, sem, out_sem = refs[GROUPS + 1 :]
    for q, piece in enumerate(pieces):

        def start(p, carry, piece=piece):
            rank = (meta_ref[p] >> 6) & 31
            pltpu.make_async_copy(piece.at[rank], held.at[p], sem).start()
            return carry

        lax.fori_loop(meta_ref[STARTS + q], meta_ref[STARTS + q + 1], start, 0)

    def wait(p, carry):
        pltpu.make_async_copy(pieces[0].at[0], held.at[0], sem).wait()
        return carry

    count = meta_ref[STARTS + GROUPS]
    lax.fori_loop(0, count, wait, 0)

    def out_copy(i):
        span = pl.ds(pl.multiple_of(i * UNROLL, UNROLL), UNROLL)
        return pltpu.make_async_copy(held.at[span], out_ref.at[span], out_sem)

    def start_out(i, carry):
        out_copy(i).start()
        return carry

    def wait_out(i, carry):
        out_copy(i).wait()
        return carry

    chunks = (count + UNROLL - 1) // UNROLL
    lax.fori_loop(0, chunks, start_out, 0)
    lax.fori_loop(0, chunks, wait_out, 0)


def pack_weights(meta, pieces):
    return pl.pallas_call(
        pack_kernel,
        out_shape=jax.ShapeDtypeStruct((LIST, BLK, BLK), BF16),
        in_specs=[smem_spec()] + [any_spec()] * GROUPS,
        out_specs=any_spec(),
        scratch_shapes=[
            pltpu.VMEM((LIST, BLK, BLK), BF16),
            pltpu.SemaphoreType.DMA,
            pltpu.SemaphoreType.DMA,
        ],
        name="pack_weights",
    )(meta, *pieces)


def make_partial_kernel(n_pieces, offset):
    def kernel(meta_ref, weight_ref, *refs):
        pieces = refs[:n_pieces]
        outs = refs[n_pieces : n_pieces + NX + 1]
        rates, weights, acc, rate_sem, weight_sem, out_sem = refs[n_pieces + NX + 1 :]
        count = meta_ref[STARTS + GROUPS]
        chunks = (count + UNROLL - 1) // UNROLL

        def weight_copy(i):
            span = pl.ds(pl.multiple_of(i * UNROLL, UNROLL), UNROLL)
            return pltpu.make_async_copy(weight_ref.at[span], weights.at[span], weight_sem)

        def start_weight(i, carry):
            weight_copy(i).start()
            return carry

        lax.fori_loop(0, chunks, start_weight, 0)
        if n_pieces == 1:

            def start_rate(p, carry):
                place = (meta_ref[p] >> 11) & 511
                pltpu.make_async_copy(
                    pieces[0].at[place + offset], rates.at[p], rate_sem
                ).start()
                return carry

            lax.fori_loop(0, count, start_rate, 0)
        else:
            for q, piece in enumerate(pieces):

                def start_rate(i, carry, piece=piece):
                    v = meta_ref[FETCH + i]
                    pltpu.make_async_copy(
                        piece.at[(v >> 8) & 63], rates.at[v & 255], rate_sem
                    ).start()
                    return carry

                lax.fori_loop(meta_ref[BOUNDS + q], meta_ref[BOUNDS + q + 1], start_rate, 0)
        acc[...] = jnp.zeros_like(acc)

        def wait_rate(p, carry):
            pltpu.make_async_copy(pieces[0].at[0], rates.at[0], rate_sem).wait()
            return carry

        def wait_weight(i, carry):
            weight_copy(i).wait()
            return carry

        lax.fori_loop(0, count, wait_rate, 0)
        lax.fori_loop(0, chunks, wait_weight, 0)

        def chunk(i, carry):
            prods = []
            for u in range(UNROLL):
                p = i * UNROLL + u
                row = jnp.where(p < count, meta_ref[p] & 63, GROUPS * ROWS)
                prod = lax.dot_general(
                    rates[p], weights[p], (((1,), (1,)), ((), ())), preferred_element_type=F32
                )
                prods.append((row, prod))
            for row, prod in prods:
                acc[row] += prod
            return carry

        lax.fori_loop(0, chunks, chunk, 0)
        copies = [
            pltpu.make_async_copy(acc.at[pl.ds(g * ROWS, ROWS)], outs[g], out_sem.at[g])
            for g in range(NX)
        ] + [
            pltpu.make_async_copy(
                acc.at[pl.ds(NX * ROWS, NX * ROWS)], outs[NX], out_sem.at[NX]
            )
        ]
        for copy in copies:
            copy.start()
        for copy in copies:
            copy.wait()

    return kernel


def partial_sums(meta, weights, pieces, offset):
    return pl.pallas_call(
        make_partial_kernel(len(pieces), offset),
        out_shape=[jax.ShapeDtypeStruct((ROWS, BLK, BLK), F32)] * NX
        + [jax.ShapeDtypeStruct((NX * ROWS, BLK, BLK), F32)],
        in_specs=[smem_spec()] + [any_spec()] * (1 + len(pieces)),
        out_specs=[any_spec()] * (NX + 1),
        scratch_shapes=[
            pltpu.VMEM((LIST, BLK, BLK), BF16),
            pltpu.VMEM((LIST, BLK, BLK), BF16),
            pltpu.VMEM((GROUPS * ROWS + 1, BLK, BLK), F32),
            pltpu.SemaphoreType.DMA,
            pltpu.SemaphoreType.DMA,
            pltpu.SemaphoreType.DMA((NX + 1,)),
        ],
        compiler_params=pltpu.CompilerParams(vmem_limit_bytes=40 * 1024 * 1024),
        name="partial_sums",
    )(meta, weights, *pieces)


def step_kernel(
    pos_ref,
    membrane_ref,
    stimulus_ref,
    leak_ref,
    weight_ref,
    f0_ref,
    f1_ref,
    f2_ref,
    f3_ref,
    *refs,
):
    pieces = refs[:GROUPS]
    out_ref, rate_ref = refs[GROUPS : GROUPS + 2]
    section, sems = refs[GROUPS + 2 :]
    copies = [
        pltpu.make_async_copy(piece, section.at[pl.ds(q * ROWS, ROWS)], sems.at[q])
        for q, piece in enumerate(pieces)
    ]
    for copy in copies:
        copy.start()
    for copy in copies:
        copy.wait()

    def row(i, carry):
        total = f0_ref[i] + f1_ref[i].astype(F32) + f2_ref[i].astype(F32) + f3_ref[i].astype(F32) + stimulus_ref[i].astype(F32)
        for k in range(0, LOCAL, 2):
            left = jnp.concatenate(
                [section[pos_ref[i * LOCAL + k]], section[pos_ref[i * LOCAL + k + 1]]], axis=1
            )
            right = jnp.concatenate([weight_ref[i, k], weight_ref[i, k + 1]], axis=1)
            total += lax.dot_general(
                left, right, (((1,), (1,)), ((), ())), preferred_element_type=F32
            )
        old = membrane_ref[i]
        new = old + leak_ref[pl.ds(i, 1), :] * (total - old)
        out_ref[i] = new
        soft = jnp.maximum(new, 0.0) + jnp.log1p(jnp.exp(-jnp.abs(new)))
        rate_ref[i] = soft.astype(BF16)
        return carry

    lax.fori_loop(0, ROWS, row, 0)


def step_of(pos, membrane, stimulus, leak, weights, far, pieces):
    return pl.pallas_call(
        step_kernel,
        out_shape=[
            jax.ShapeDtypeStruct((ROWS, BLK, BLK), F32),
            jax.ShapeDtypeStruct((ROWS, BLK, BLK), BF16),
        ],
        in_specs=[smem_spec()] + [vmem_spec()] * 8 + [any_spec()] * GROUPS,
        out_specs=[vmem_spec()] * 2,
        scratch_shapes=[
            pltpu.VMEM((SEC, BLK, BLK), BF16),
            pltpu.SemaphoreType.DMA((GROUPS,)),
        ],
        compiler_params=pltpu.CompilerParams(vmem_limit_bytes=24 * 1024 * 1024),
        name="step",
    )(pos, membrane, stimulus, leak, weights, *far, *pieces)


def after(value, *deps):
    return lax.optimization_barrier((value, *deps))[0]


def gather_plane(frame, beside):
    a0, b0 = frame[:NA], frame[NA:]
    p1, p3, p2 = shift(b0, "y", 1), shift(b0, "y", -1), shift(b0, "y", 2)
    f1, g1 = shift(a0, "z", 1), shift(a0, "z", -1)
    first = jnp.concatenate([a0, f1, g1], axis=0)
    f2, g2 = shift(f1, "z", 1), shift(g1, "z", -1)
    f3, g3 = shift(f2, "z", 1), shift(g2, "z", -1)
    f4 = shift(f3, "z", 1)
    first, p1, p2, p3 = lax.optimization_barrier((first, p1, p2, p3))
    yb = jnp.concatenate([b0, p1, p2, p3], axis=0)
    u1, v1 = shift(first, "y", 1), shift(first, "y", -1)
    fs, gs = [yb], [yb]
    for _ in range(4):
        fs.append(shift(fs[-1], "z", 1))
    for _ in range(3):
        gs.append(shift(gs[-1], "z", -1))
    second = jnp.concatenate([f2, g2, f3, g3, f4], axis=0)
    second, u1, v1 = lax.optimization_barrier((second, u1, v1, *beside))[:3]
    u2, v2 = shift(second, "y", 1), shift(second, "y", -1)
    h1, h2 = (3 * NA + 1) // 2, (5 * NA + 1) // 2
    w11, w12 = shift(u1[:h1], "y", 1), shift(v1[h1:], "y", -1)
    w11, w12, u2, v2 = lax.optimization_barrier((w11, w12, u2, v2))
    w21, w22 = shift(u2[:h2], "y", 1), shift(v2[h2:], "y", -1)
    return [first, second, u1, u2, v1, v2, w11, w12, w21, w22, *fs, *gs[1:]]


EARLY, LATE = 0, 7


def lookup(index, table):
    return sum(jnp.where(index == i, v, 0) for i, v in enumerate(table))


def place_of(ez, ey, j):
    h1, h2 = (3 * NA + 1) // 2, (5 * NA + 1) // 2
    late = ((ez >= 2) & (ez <= 6)).astype(jnp.int32)
    off = lookup(ez, [0, 1, 0, 2, 4, 3, 1, 2]) * NA + j
    half = jnp.where(late == 1, h2, h1)
    upper = off >= half
    piece_a = jnp.where(
        ey == 2,
        6 + 2 * late + upper.astype(jnp.int32),
        lookup(ey, [0, 2, 0, 4]) + late,
    )
    off_a = jnp.where((ey == 2) & upper, off - half, off)
    piece_b = lookup(ez, [10, 11, 12, 13, 14, 17, 16, 15])
    off_b = ey * NB + j - NA
    in_a = j < NA
    return jnp.where(in_a, piece_a, piece_b), jnp.where(in_a, off_a, off_b)


def total_of(mask, axis=-1):
    return jnp.sum(mask, axis=axis, dtype=jnp.int32)


def shards(
    initial_state,
    past_rates,
    stimulus,
    leak_rate,
    local_weight,
    far_weight,
    local_index,
    area_sizes,
    far_area,
    far_offset,
):
    x, z, y, c = (lax.axis_index(n) for n in ("x", "z", "y", "c"))
    first_rate = jax.nn.softplus(initial_state).astype(BF16)

    def section_of(rate):
        parts = [rate] + [shift(rate, "y", g) for g in range(1, NY)]
        return parts + [swap(p) for p in parts]

    section = section_of(first_rate)
    plane0 = gather_plane(past_rates[0], section)
    both = lax.all_gather(
        after(jnp.concatenate([past_rates[1], first_rate], axis=0), plane0[2]),
        ("z", "y"),
        axis=0,
        tiled=True,
    )

    def mine(table):
        t = table.reshape(NX, NZ, NY, NC, LINKS)
        t = lax.dynamic_index_in_dim(t, z, 1, keepdims=False)
        return lax.dynamic_index_in_dim(t, y, 1, keepdims=False)

    area, offset = mine(far_area), mine(far_offset)
    ids = jnp.arange(area_sizes.shape[0], dtype=jnp.int32)
    starts = jnp.sum(jnp.where(ids[None, :] < ids[:, None], area_sizes[None, :], 0), axis=-1)
    match = area[..., None] == ids
    area_len = jnp.sum(jnp.where(match, area_sizes, 0), axis=-1)
    first = jnp.sum(jnp.where(match, starts, 0), axis=-1)
    block = first * SEC + offset % (area_len * SEC)
    plane = block >> 9
    lids = jnp.arange(LINKS, dtype=jnp.int32)
    earlier = lids[None, :] < lids[:, None]
    rank = total_of((plane[..., :, None] == plane[..., None, :]) & earlier)

    own = lambda t: lax.dynamic_index_in_dim(
        lax.dynamic_index_in_dim(t, x, 0, keepdims=False), c, 0, keepdims=False
    )
    own_plane, own_rank = own(plane), own(rank)
    hop = jnp.arange(NX, dtype=jnp.int32)
    slot = jnp.arange(CAP, dtype=jnp.int32)
    fits = (own_plane == ((x + hop) & 3)[:, None])[:, None, :] & (
        own_rank[None, None, :] == slot[None, :, None]
    )
    pick = after(jnp.sum(jnp.where(fits, lids, 0), axis=-1), plane0[EARLY])
    flat_weight = far_weight.reshape(LINKS, BLK, BLK)
    near = [flat_weight[pick[0]]] + [
        shift(flat_weight[pick[g]], "x", g) for g in range(1, NX)
    ]

    dest_x = jnp.arange(NX, dtype=jnp.int32)[:, None, None]
    dest_c = jnp.arange(NC, dtype=jnp.int32)[None, :, None]
    group = jnp.where(dest_c == c, 0, NX) + ((x - dest_x) & 3) + 0 * plane
    source_z, source_y, source_j = (block >> 6) & 7, (block >> 4) & 3, block & 7
    piece, off = place_of((z - source_z) & 7, (y - source_y) & 3, source_j)
    flat = lambda t: t.reshape(-1)
    works = flat((plane == x) & (((block >> 3) & 1) == c))
    order = flat(group * LINKS + lids)
    before = total_of(works[None, :] & (order[None, :] < order[:, None]))
    value = flat(
        group * ROWS + lids // FAR + (rank << 6) + ((source_z * 64 + source_y * 16 + source_j) << 11)
    )
    spots = jnp.arange(LIST, dtype=jnp.int32)
    links = jnp.sum(
        jnp.where(works[None, :] & (before[None, :] == spots[:, None]), value[None, :], 0), axis=-1
    )
    fetch_order = flat(piece) * 512 + order
    fetch_before = total_of(works[None, :] & (fetch_order[None, :] < fetch_order[:, None]))
    fetch_value = before + (flat(off) << 8)
    fetch = jnp.sum(
        jnp.where(
            works[None, :] & (fetch_before[None, :] == spots[:, None]), fetch_value[None, :], 0
        ),
        axis=-1,
    )
    group_starts = total_of(
        works[None, :] & (flat(group)[None, :] < jnp.arange(GROUPS + 1, dtype=jnp.int32)[:, None])
    )
    piece_starts = total_of(
        works[None, :] & (flat(piece)[None, :] < jnp.arange(PIECES + 1, dtype=jnp.int32)[:, None])
    )
    meta = jnp.concatenate([links, fetch, group_starts, piece_starts])
    weights = pack_weights(meta, near + [swap(w) for w in near])

    col = local_index >> 3
    local_pos = (
        jnp.where((col & 1) == c, 0, 32) + ((y - (col >> 1)) & 3) * 8 + (local_index & 7)
    ).reshape(-1)

    def far_input(pieces, offset):
        *kept, other = partial_sums(meta, weights, pieces, offset)
        other = swap(other).reshape(NX, ROWS, BLK, BLK)
        sums = [kept[g] + other[g] for g in range(NX)]
        return [sums[0]] + [shift(sums[g].astype(BF16), "x", -g) for g in range(1, NX)]

    membrane, rate = initial_state, first_rate
    far = [far_input(plane0, 0), None, None, None]
    for step in range(STEPS):
        if step == 1:
            waited = after(both, plane3[LATE + 1])
            far[1], far[2] = far_input([waited], 0), far_input([waited], ROWS)
        membrane, rate = step_of(
            local_pos, membrane, stimulus, leak_rate, local_weight, far[step], section
        )
        if step == 0:
            section = section_of(rate)
            plane3 = gather_plane(rate, section)
        elif step < 3:
            section = section_of(rate)
        if step == 1:
            far[3] = far_input(plane3, 0)
    return membrane


def solution(mesh):
    mesh4 = Mesh(mesh.devices.reshape(NX, NZ, NY, NC), ("x", "z", "y", "c"))
    dev = ("x", "z", "y", "c")
    return jax.shard_map(
        shards,
        mesh=mesh4,
        in_specs=(
            P(dev, None, None),
            P(None, dev, None, None),
            P(dev, None, None),
            P(dev, None),
            P(dev, None, None, None),
            P(dev, None, None, None),
            P(dev, None),
            P(),
            P(),
            P(),
        ),
        out_specs=P(dev, None, None),
        check_vma=False,
    )
```

```python
import jax
import jax.numpy as jnp
from jax import lax
from jax.experimental import pallas as pl
from jax.experimental.pallas import tpu as pltpu
from jax.sharding import Mesh, PartitionSpec as P

STEPS = 4
NX, NZ, NY, NC = 4, 8, 4, 2
ROWS = 8
LOCAL = 12
FAR = 8
LINKS = ROWS * FAR
BLK = 128
SEC = 64
CAP = 32
GROUPS = 2 * NX
LIST = GROUPS * CAP
UNROLL = 8
NA = 5
NB = ROWS - NA
PIECES = 18
F32 = jnp.float32
BF16 = jnp.bfloat16
FETCH = LIST
STARTS = 2 * LIST
BOUNDS = STARTS + GROUPS + 1


def ring(n, shift):
    return [(i, (i + shift) % n) for i in range(n)]


def shift(a, axis, by):
    return lax.ppermute(a, axis, ring({"x": NX, "y": NY, "z": NZ}[axis], by))


def swap(a):
    return lax.ppermute(a, "c", [(0, 1), (1, 0)])


def any_spec():
    return pl.BlockSpec(memory_space=pl.ANY)


def vmem_spec():
    return pl.BlockSpec(memory_space=pltpu.VMEM)


def smem_spec():
    return pl.BlockSpec(memory_space=pltpu.SMEM)


def pack_kernel(meta_ref, *refs):
    pieces, out_ref = refs[:GROUPS], refs[GROUPS]
    held, sem, out_sem = refs[GROUPS + 1 :]
    for q, piece in enumerate(pieces):

        def start(p, carry, piece=piece):
            rank = (meta_ref[p] >> 6) & 31
            pltpu.make_async_copy(piece.at[rank], held.at[p], sem).start()
            return carry

        lax.fori_loop(meta_ref[STARTS + q], meta_ref[STARTS + q + 1], start, 0)

    def wait(p, carry):
        pltpu.make_async_copy(pieces[0].at[0], held.at[0], sem).wait()
        return carry

    count = meta_ref[STARTS + GROUPS]
    lax.fori_loop(0, count, wait, 0)

    def out_copy(i):
        span = pl.ds(pl.multiple_of(i * UNROLL, UNROLL), UNROLL)
        return pltpu.make_async_copy(held.at[span], out_ref.at[span], out_sem)

    def start_out(i, carry):
        out_copy(i).start()
        return carry

    def wait_out(i, carry):
        out_copy(i).wait()
        return carry

    chunks = (count + UNROLL - 1) // UNROLL
    lax.fori_loop(0, chunks, start_out, 0)
    lax.fori_loop(0, chunks, wait_out, 0)


def pack_weights(meta, pieces):
    return pl.pallas_call(
        pack_kernel,
        out_shape=jax.ShapeDtypeStruct((LIST, BLK, BLK), BF16),
        in_specs=[smem_spec()] + [any_spec()] * GROUPS,
        out_specs=any_spec(),
        scratch_shapes=[
            pltpu.VMEM((LIST, BLK, BLK), BF16),
            pltpu.SemaphoreType.DMA,
            pltpu.SemaphoreType.DMA,
        ],
        name="pack_weights",
    )(meta, *pieces)


def make_partial_kernel(n_pieces, offset):
    def kernel(meta_ref, weight_ref, *refs):
        pieces = refs[:n_pieces]
        outs = refs[n_pieces : n_pieces + NX + 1]
        rates, weights, acc, rate_sem, weight_sem, out_sem = refs[n_pieces + NX + 1 :]
        count = meta_ref[STARTS + GROUPS]
        chunks = (count + UNROLL - 1) // UNROLL

        def weight_copy(i):
            span = pl.ds(pl.multiple_of(i * UNROLL, UNROLL), UNROLL)
            return pltpu.make_async_copy(weight_ref.at[span], weights.at[span], weight_sem)

        def start_weight(i, carry):
            weight_copy(i).start()
            return carry

        lax.fori_loop(0, chunks, start_weight, 0)
        if n_pieces == 1:

            def start_rate(p, carry):
                place = (meta_ref[p] >> 11) & 511
                pltpu.make_async_copy(
                    pieces[0].at[place + offset], rates.at[p], rate_sem
                ).start()
                return carry

            lax.fori_loop(0, count, start_rate, 0)
        else:
            for q, piece in enumerate(pieces):

                def start_rate(i, carry, piece=piece):
                    v = meta_ref[FETCH + i]
                    pltpu.make_async_copy(
                        piece.at[(v >> 8) & 63], rates.at[v & 255], rate_sem
                    ).start()
                    return carry

                lax.fori_loop(meta_ref[BOUNDS + q], meta_ref[BOUNDS + q + 1], start_rate, 0)
        acc[...] = jnp.zeros_like(acc)

        def wait_rate(p, carry):
            pltpu.make_async_copy(pieces[0].at[0], rates.at[0], rate_sem).wait()
            return carry

        def wait_weight(i, carry):
            weight_copy(i).wait()
            return carry

        lax.fori_loop(0, count, wait_rate, 0)
        lax.fori_loop(0, chunks, wait_weight, 0)

        def chunk(i, carry):
            prods = []
            for u in range(UNROLL):
                p = i * UNROLL + u
                row = jnp.where(p < count, meta_ref[p] & 63, GROUPS * ROWS)
                prod = lax.dot_general(
                    rates[p], weights[p], (((1,), (1,)), ((), ())), preferred_element_type=F32
                )
                prods.append((row, prod))
            for row, prod in prods:
                acc[row] += prod
            return carry

        lax.fori_loop(0, chunks, chunk, 0)
        copies = [
            pltpu.make_async_copy(acc.at[pl.ds(g * ROWS, ROWS)], outs[g], out_sem.at[g])
            for g in range(NX)
        ] + [
            pltpu.make_async_copy(
                acc.at[pl.ds(NX * ROWS, NX * ROWS)], outs[NX], out_sem.at[NX]
            )
        ]
        for copy in copies:
            copy.start()
        for copy in copies:
            copy.wait()

    return kernel


def partial_sums(meta, weights, pieces, offset):
    return pl.pallas_call(
        make_partial_kernel(len(pieces), offset),
        out_shape=[jax.ShapeDtypeStruct((ROWS, BLK, BLK), F32)] * NX
        + [jax.ShapeDtypeStruct((NX * ROWS, BLK, BLK), F32)],
        in_specs=[smem_spec()] + [any_spec()] * (1 + len(pieces)),
        out_specs=[any_spec()] * (NX + 1),
        scratch_shapes=[
            pltpu.VMEM((LIST, BLK, BLK), BF16),
            pltpu.VMEM((LIST, BLK, BLK), BF16),
            pltpu.VMEM((GROUPS * ROWS + 1, BLK, BLK), F32),
            pltpu.SemaphoreType.DMA,
            pltpu.SemaphoreType.DMA,
            pltpu.SemaphoreType.DMA((NX + 1,)),
        ],
        compiler_params=pltpu.CompilerParams(vmem_limit_bytes=40 * 1024 * 1024),
        name="partial_sums",
    )(meta, weights, *pieces)


def step_kernel(
    pos_ref,
    membrane_ref,
    stimulus_ref,
    leak_ref,
    weight_ref,
    f0_ref,
    f1_ref,
    f2_ref,
    f3_ref,
    *refs,
):
    pieces = refs[:GROUPS]
    out_ref, rate_ref = refs[GROUPS : GROUPS + 2]
    section, sems = refs[GROUPS + 2 :]
    copies = [
        pltpu.make_async_copy(piece, section.at[pl.ds(q * ROWS, ROWS)], sems.at[q])
        for q, piece in enumerate(pieces)
    ]
    for copy in copies:
        copy.start()
    for copy in copies:
        copy.wait()

    def row(i, carry):
        total = f0_ref[i] + f1_ref[i].astype(F32) + f2_ref[i].astype(F32) + f3_ref[i].astype(F32) + stimulus_ref[i].astype(F32)
        for k in range(0, LOCAL, 2):
            left = jnp.concatenate(
                [section[pos_ref[i * LOCAL + k]], section[pos_ref[i * LOCAL + k + 1]]], axis=1
            )
            right = jnp.concatenate([weight_ref[i, k], weight_ref[i, k + 1]], axis=1)
            total += lax.dot_general(
                left, right, (((1,), (1,)), ((), ())), preferred_element_type=F32
            )
        old = membrane_ref[i]
        new = old + leak_ref[pl.ds(i, 1), :] * (total - old)
        out_ref[i] = new
        soft = jnp.maximum(new, 0.0) + jnp.log1p(jnp.exp(-jnp.abs(new)))
        rate_ref[i] = soft.astype(BF16)
        return carry

    lax.fori_loop(0, ROWS, row, 0)


def step_of(pos, membrane, stimulus, leak, weights, far, pieces):
    return pl.pallas_call(
        step_kernel,
        out_shape=[
            jax.ShapeDtypeStruct((ROWS, BLK, BLK), F32),
            jax.ShapeDtypeStruct((ROWS, BLK, BLK), BF16),
        ],
        in_specs=[smem_spec()] + [vmem_spec()] * 8 + [any_spec()] * GROUPS,
        out_specs=[vmem_spec()] * 2,
        scratch_shapes=[
            pltpu.VMEM((SEC, BLK, BLK), BF16),
            pltpu.SemaphoreType.DMA((GROUPS,)),
        ],
        compiler_params=pltpu.CompilerParams(vmem_limit_bytes=24 * 1024 * 1024),
        name="step",
    )(pos, membrane, stimulus, leak, weights, *far, *pieces)


def after(value, *deps):
    return lax.optimization_barrier((value, *deps))[0]


def gather_plane(frame, beside):
    a0, b0 = frame[:NA], frame[NA:]
    p1, p3, p2 = shift(b0, "y", 1), shift(b0, "y", -1), shift(b0, "y", 2)
    f1, g1 = shift(a0, "z", 1), shift(a0, "z", -1)
    first = jnp.concatenate([a0, f1, g1], axis=0)
    first, p1, p2, p3, f1, g1 = lax.optimization_barrier((first, p1, p2, p3, f1, g1))
    yb = jnp.concatenate([b0, p1, p2, p3], axis=0)
    k1, m1 = shift(yb, "z", 1), shift(yb, "z", -1)
    f2, g2 = shift(f1, "z", 1), shift(g1, "z", -1)
    u1, v1 = shift(first, "y", 1), shift(first, "y", -1)
    f3, g3 = shift(f2, "z", 1), shift(g2, "z", -1)
    k1, m1, f3, g3 = lax.optimization_barrier((k1, m1, f3, g3))
    k2, m2 = shift(k1, "z", 1), shift(m1, "z", -1)
    f4 = shift(f3, "z", 1)
    second = jnp.concatenate([f2, g2, f3, g3, f4], axis=0)
    second, u1, v1 = lax.optimization_barrier((second, u1, v1, *beside))[:3]
    h1, h2 = (3 * NA + 1) // 2, (5 * NA + 1) // 2
    u2, v2 = shift(second, "y", 1), shift(second, "y", -1)
    w11, w12 = shift(u1[:h1], "y", 1), shift(v1[h1:], "y", -1)
    k3, m3 = shift(k2, "z", 1), shift(m2, "z", -1)
    w11, w12, u2, v2, k3, m3 = lax.optimization_barrier((w11, w12, u2, v2, k3, m3))
    k4 = shift(k3, "z", 1)
    w21, w22 = shift(u2[:h2], "y", 1), shift(v2[h2:], "y", -1)
    return [
        first, second, u1, u2, v1, v2, w11, w12, w21, w22, yb, k1, k2, k3, k4, m1, m2, m3
    ]


EARLY, LATE = 0, 7


def lookup(index, table):
    return sum(jnp.where(index == i, v, 0) for i, v in enumerate(table))


def place_of(ez, ey, j):
    h1, h2 = (3 * NA + 1) // 2, (5 * NA + 1) // 2
    late = ((ez >= 2) & (ez <= 6)).astype(jnp.int32)
    off = lookup(ez, [0, 1, 0, 2, 4, 3, 1, 2]) * NA + j
    half = jnp.where(late == 1, h2, h1)
    upper = off >= half
    piece_a = jnp.where(
        ey == 2,
        6 + 2 * late + upper.astype(jnp.int32),
        lookup(ey, [0, 2, 0, 4]) + late,
    )
    off_a = jnp.where((ey == 2) & upper, off - half, off)
    piece_b = lookup(ez, [10, 11, 12, 13, 14, 17, 16, 15])
    off_b = ey * NB + j - NA
    in_a = j < NA
    return jnp.where(in_a, piece_a, piece_b), jnp.where(in_a, off_a, off_b)


def total_of(mask, axis=-1):
    return jnp.sum(mask, axis=axis, dtype=jnp.int32)


def shards(
    initial_state,
    past_rates,
    stimulus,
    leak_rate,
    local_weight,
    far_weight,
    local_index,
    area_sizes,
    far_area,
    far_offset,
):
    x, z, y, c = (lax.axis_index(n) for n in ("x", "z", "y", "c"))
    first_rate = jax.nn.softplus(initial_state).astype(BF16)

    def section_of(rate):
        parts = [rate] + [shift(rate, "y", g) for g in range(1, NY)]
        return parts + [swap(p) for p in parts]

    section = section_of(first_rate)
    plane0 = gather_plane(past_rates[0], section)
    both = lax.all_gather(
        after(jnp.concatenate([past_rates[1], first_rate], axis=0), plane0[2]),
        ("z", "y"),
        axis=0,
        tiled=True,
    )

    def mine(table):
        t = table.reshape(NX, NZ, NY, NC, LINKS)
        t = lax.dynamic_index_in_dim(t, z, 1, keepdims=False)
        return lax.dynamic_index_in_dim(t, y, 1, keepdims=False)

    area, offset = mine(far_area), mine(far_offset)
    ids = jnp.arange(area_sizes.shape[0], dtype=jnp.int32)
    starts = jnp.sum(jnp.where(ids[None, :] < ids[:, None], area_sizes[None, :], 0), axis=-1)
    match = area[..., None] == ids
    area_len = jnp.sum(jnp.where(match, area_sizes, 0), axis=-1)
    first = jnp.sum(jnp.where(match, starts, 0), axis=-1)
    block = first * SEC + offset % (area_len * SEC)
    plane = block >> 9
    lids = jnp.arange(LINKS, dtype=jnp.int32)
    earlier = lids[None, :] < lids[:, None]
    rank = total_of((plane[..., :, None] == plane[..., None, :]) & earlier)

    own = lambda t: lax.dynamic_index_in_dim(
        lax.dynamic_index_in_dim(t, x, 0, keepdims=False), c, 0, keepdims=False
    )
    own_plane, own_rank = own(plane), own(rank)
    hop = jnp.arange(NX, dtype=jnp.int32)
    slot = jnp.arange(CAP, dtype=jnp.int32)
    fits = (own_plane == ((x + hop) & 3)[:, None])[:, None, :] & (
        own_rank[None, None, :] == slot[None, :, None]
    )
    pick = after(jnp.sum(jnp.where(fits, lids, 0), axis=-1), plane0[EARLY])
    flat_weight = far_weight.reshape(LINKS, BLK, BLK)
    near = [flat_weight[pick[0]]] + [
        shift(flat_weight[pick[g]], "x", g) for g in range(1, NX)
    ]

    dest_x = jnp.arange(NX, dtype=jnp.int32)[:, None, None]
    dest_c = jnp.arange(NC, dtype=jnp.int32)[None, :, None]
    group = jnp.where(dest_c == c, 0, NX) + ((x - dest_x) & 3) + 0 * plane
    source_z, source_y, source_j = (block >> 6) & 7, (block >> 4) & 3, block & 7
    piece, off = place_of((z - source_z) & 7, (y - source_y) & 3, source_j)
    flat = lambda t: t.reshape(-1)
    works = flat((plane == x) & (((block >> 3) & 1) == c))
    order = flat(group * LINKS + lids)
    before = total_of(works[None, :] & (order[None, :] < order[:, None]))
    value = flat(
        group * ROWS + lids // FAR + (rank << 6) + ((source_z * 64 + source_y * 16 + source_j) << 11)
    )
    spots = jnp.arange(LIST, dtype=jnp.int32)
    links = jnp.sum(
        jnp.where(works[None, :] & (before[None, :] == spots[:, None]), value[None, :], 0), axis=-1
    )
    fetch_order = flat(piece) * 512 + order
    fetch_before = total_of(works[None, :] & (fetch_order[None, :] < fetch_order[:, None]))
    fetch_value = before + (flat(off) << 8)
    fetch = jnp.sum(
        jnp.where(
            works[None, :] & (fetch_before[None, :] == spots[:, None]), fetch_value[None, :], 0
        ),
        axis=-1,
    )
    group_starts = total_of(
        works[None, :] & (flat(group)[None, :] < jnp.arange(GROUPS + 1, dtype=jnp.int32)[:, None])
    )
    piece_starts = total_of(
        works[None, :] & (flat(piece)[None, :] < jnp.arange(PIECES + 1, dtype=jnp.int32)[:, None])
    )
    meta = jnp.concatenate([links, fetch, group_starts, piece_starts])
    weights = pack_weights(meta, near + [swap(w) for w in near])

    col = local_index >> 3
    local_pos = (
        jnp.where((col & 1) == c, 0, 32) + ((y - (col >> 1)) & 3) * 8 + (local_index & 7)
    ).reshape(-1)

    def far_input(pieces, offset):
        *kept, other = partial_sums(meta, weights, pieces, offset)
        other = swap(other).reshape(NX, ROWS, BLK, BLK)
        sums = [kept[g] + other[g] for g in range(NX)]
        return [sums[0]] + [shift(sums[g].astype(BF16), "x", -g) for g in range(1, NX)]

    membrane, rate = initial_state, first_rate
    far = [far_input(plane0, 0), None, None, None]
    for step in range(STEPS):
        if step == 1:
            waited = after(both, plane3[12])
            far[1], far[2] = far_input([waited], 0), far_input([waited], ROWS)
        membrane, rate = step_of(
            local_pos, membrane, stimulus, leak_rate, local_weight, far[step], section
        )
        if step == 0:
            section = section_of(rate)
            plane3 = gather_plane(rate, section)
        elif step < 3:
            section = section_of(rate)
        if step == 1:
            plane3[LATE + 1] = after(plane3[LATE + 1], rate)
            far[3] = far_input(plane3, 0)
    return membrane


def solution(mesh):
    mesh4 = Mesh(mesh.devices.reshape(NX, NZ, NY, NC), ("x", "z", "y", "c"))
    dev = ("x", "z", "y", "c")
    return jax.shard_map(
        shards,
        mesh=mesh4,
        in_specs=(
            P(dev, None, None),
            P(None, dev, None, None),
            P(dev, None, None),
            P(dev, None),
            P(dev, None, None, None),
            P(dev, None, None, None),
            P(dev, None),
            P(),
            P(),
            P(),
        ),
        out_specs=P(dev, None, None),
        check_vma=False,
    )
```

```python
import jax
import jax.numpy as jnp
from jax import lax
from jax.experimental import pallas as pl
from jax.experimental.pallas import tpu as pltpu
from jax.sharding import Mesh, PartitionSpec as P

STEPS = 4
NX, NZ, NY, NC = 4, 8, 4, 2
ROWS = 8
LOCAL = 12
FAR = 8
LINKS = ROWS * FAR
BLK = 128
SEC = 64
CAP = 32
GROUPS = 2 * NX
LIST = GROUPS * CAP
UNROLL = 8
NA = 5
NB = ROWS - NA
PIECES = 18
F32 = jnp.float32
BF16 = jnp.bfloat16
FETCH = LIST
STARTS = 2 * LIST
BOUNDS = STARTS + GROUPS + 1


def ring(n, shift):
    return [(i, (i + shift) % n) for i in range(n)]


def shift(a, axis, by):
    return lax.ppermute(a, axis, ring({"x": NX, "y": NY, "z": NZ}[axis], by))


def swap(a):
    return lax.ppermute(a, "c", [(0, 1), (1, 0)])


def any_spec():
    return pl.BlockSpec(memory_space=pl.ANY)


def vmem_spec():
    return pl.BlockSpec(memory_space=pltpu.VMEM)


def smem_spec():
    return pl.BlockSpec(memory_space=pltpu.SMEM)


def pack_kernel(meta_ref, *refs):
    pieces, out_ref = refs[:GROUPS], refs[GROUPS]
    held, sem, out_sem = refs[GROUPS + 1 :]
    for q, piece in enumerate(pieces):

        def start(p, carry, piece=piece):
            rank = (meta_ref[p] >> 6) & 31
            pltpu.make_async_copy(piece.at[rank], held.at[p], sem).start()
            return carry

        lax.fori_loop(meta_ref[STARTS + q], meta_ref[STARTS + q + 1], start, 0)

    def wait(p, carry):
        pltpu.make_async_copy(pieces[0].at[0], held.at[0], sem).wait()
        return carry

    count = meta_ref[STARTS + GROUPS]
    lax.fori_loop(0, count, wait, 0)

    def out_copy(i):
        span = pl.ds(pl.multiple_of(i * UNROLL, UNROLL), UNROLL)
        return pltpu.make_async_copy(held.at[span], out_ref.at[span], out_sem)

    def start_out(i, carry):
        out_copy(i).start()
        return carry

    def wait_out(i, carry):
        out_copy(i).wait()
        return carry

    chunks = (count + UNROLL - 1) // UNROLL
    lax.fori_loop(0, chunks, start_out, 0)
    lax.fori_loop(0, chunks, wait_out, 0)


def pack_weights(meta, pieces):
    return pl.pallas_call(
        pack_kernel,
        out_shape=jax.ShapeDtypeStruct((LIST, BLK, BLK), BF16),
        in_specs=[smem_spec()] + [any_spec()] * GROUPS,
        out_specs=any_spec(),
        scratch_shapes=[
            pltpu.VMEM((LIST, BLK, BLK), BF16),
            pltpu.SemaphoreType.DMA,
            pltpu.SemaphoreType.DMA,
        ],
        name="pack_weights",
    )(meta, *pieces)


def make_partial_kernel(n_pieces, offset):
    def kernel(meta_ref, weight_ref, *refs):
        pieces = refs[:n_pieces]
        outs = refs[n_pieces : n_pieces + NX + 1]
        rates, weights, acc, rate_sem, weight_sem, out_sem = refs[n_pieces + NX + 1 :]
        count = meta_ref[STARTS + GROUPS]
        chunks = (count + UNROLL - 1) // UNROLL

        def weight_copy(i):
            span = pl.ds(pl.multiple_of(i * UNROLL, UNROLL), UNROLL)
            return pltpu.make_async_copy(weight_ref.at[span], weights.at[span], weight_sem)

        def start_weight(i, carry):
            weight_copy(i).start()
            return carry

        lax.fori_loop(0, chunks, start_weight, 0)
        if n_pieces == 1:

            def start_rate(p, carry):
                place = (meta_ref[p] >> 11) & 511
                pltpu.make_async_copy(
                    pieces[0].at[place + offset], rates.at[p], rate_sem
                ).start()
                return carry

            lax.fori_loop(0, count, start_rate, 0)
        else:
            for q, piece in enumerate(pieces):

                def start_rate(i, carry, piece=piece):
                    v = meta_ref[FETCH + i]
                    pltpu.make_async_copy(
                        piece.at[(v >> 8) & 63], rates.at[v & 255], rate_sem
                    ).start()
                    return carry

                lax.fori_loop(meta_ref[BOUNDS + q], meta_ref[BOUNDS + q + 1], start_rate, 0)
        acc[...] = jnp.zeros_like(acc)

        def wait_rate(p, carry):
            pltpu.make_async_copy(pieces[0].at[0], rates.at[0], rate_sem).wait()
            return carry

        def wait_weight(i, carry):
            weight_copy(i).wait()
            return carry

        lax.fori_loop(0, count, wait_rate, 0)
        lax.fori_loop(0, chunks, wait_weight, 0)

        def chunk(i, carry):
            prods = []
            for u in range(UNROLL):
                p = i * UNROLL + u
                row = jnp.where(p < count, meta_ref[p] & 63, GROUPS * ROWS)
                prod = lax.dot_general(
                    rates[p], weights[p], (((1,), (1,)), ((), ())), preferred_element_type=F32
                )
                prods.append((row, prod))
            for row, prod in prods:
                acc[row] += prod
            return carry

        lax.fori_loop(0, chunks, chunk, 0)
        copies = [
            pltpu.make_async_copy(acc.at[pl.ds(g * ROWS, ROWS)], outs[g], out_sem.at[g])
            for g in range(NX)
        ] + [
            pltpu.make_async_copy(
                acc.at[pl.ds(NX * ROWS, NX * ROWS)], outs[NX], out_sem.at[NX]
            )
        ]
        for copy in copies:
            copy.start()
        for copy in copies:
            copy.wait()

    return kernel


def partial_sums(meta, weights, pieces, offset):
    return pl.pallas_call(
        make_partial_kernel(len(pieces), offset),
        out_shape=[jax.ShapeDtypeStruct((ROWS, BLK, BLK), F32)] * NX
        + [jax.ShapeDtypeStruct((NX * ROWS, BLK, BLK), F32)],
        in_specs=[smem_spec()] + [any_spec()] * (1 + len(pieces)),
        out_specs=[any_spec()] * (NX + 1),
        scratch_shapes=[
            pltpu.VMEM((LIST, BLK, BLK), BF16),
            pltpu.VMEM((LIST, BLK, BLK), BF16),
            pltpu.VMEM((GROUPS * ROWS + 1, BLK, BLK), F32),
            pltpu.SemaphoreType.DMA,
            pltpu.SemaphoreType.DMA,
            pltpu.SemaphoreType.DMA((NX + 1,)),
        ],
        compiler_params=pltpu.CompilerParams(vmem_limit_bytes=40 * 1024 * 1024),
        name="partial_sums",
    )(meta, weights, *pieces)


def step_kernel(
    pos_ref,
    membrane_ref,
    stimulus_ref,
    leak_ref,
    weight_ref,
    f0_ref,
    f1_ref,
    f2_ref,
    f3_ref,
    *refs,
):
    pieces = refs[:GROUPS]
    out_ref, rate_ref = refs[GROUPS : GROUPS + 2]
    section, sems = refs[GROUPS + 2 :]
    copies = [
        pltpu.make_async_copy(piece, section.at[pl.ds(q * ROWS, ROWS)], sems.at[q])
        for q, piece in enumerate(pieces)
    ]
    for copy in copies:
        copy.start()
    for copy in copies:
        copy.wait()

    def row(i, carry):
        total = f0_ref[i] + f1_ref[i].astype(F32) + f2_ref[i].astype(F32) + f3_ref[i].astype(F32) + stimulus_ref[i].astype(F32)
        for k in range(0, LOCAL, 2):
            left = jnp.concatenate(
                [section[pos_ref[i * LOCAL + k]], section[pos_ref[i * LOCAL + k + 1]]], axis=1
            )
            right = jnp.concatenate([weight_ref[i, k], weight_ref[i, k + 1]], axis=1)
            total += lax.dot_general(
                left, right, (((1,), (1,)), ((), ())), preferred_element_type=F32
            )
        old = membrane_ref[i]
        new = old + leak_ref[pl.ds(i, 1), :] * (total - old)
        out_ref[i] = new
        soft = jnp.maximum(new, 0.0) + jnp.log1p(jnp.exp(-jnp.abs(new)))
        rate_ref[i] = soft.astype(BF16)
        return carry

    lax.fori_loop(0, ROWS, row, 0)


def step_of(pos, membrane, stimulus, leak, weights, far, pieces):
    return pl.pallas_call(
        step_kernel,
        out_shape=[
            jax.ShapeDtypeStruct((ROWS, BLK, BLK), F32),
            jax.ShapeDtypeStruct((ROWS, BLK, BLK), BF16),
        ],
        in_specs=[smem_spec()] + [vmem_spec()] * 8 + [any_spec()] * GROUPS,
        out_specs=[vmem_spec()] * 2,
        scratch_shapes=[
            pltpu.VMEM((SEC, BLK, BLK), BF16),
            pltpu.SemaphoreType.DMA((GROUPS,)),
        ],
        compiler_params=pltpu.CompilerParams(vmem_limit_bytes=24 * 1024 * 1024),
        name="step",
    )(pos, membrane, stimulus, leak, weights, *far, *pieces)


def after(value, *deps):
    return lax.optimization_barrier((value, *deps))[0]


def gather_plane(frame, before, beside):
    a0, b0 = frame[:NA], frame[NA:]
    p1, p3, p2 = shift(b0, "y", 1), shift(b0, "y", -1), shift(b0, "y", 2)
    f1, g1 = shift(a0, "z", 1), shift(a0, "z", -1)
    first = jnp.concatenate([a0, f1, g1], axis=0)
    f2, g2 = shift(f1, "z", 1), shift(g1, "z", -1)
    f3, g3 = shift(f2, "z", 1), shift(g2, "z", -1)
    f4 = shift(f3, "z", 1)
    first, p1, p2, p3 = lax.optimization_barrier((first, p1, p2, p3, *before))[:4]
    yb = jnp.concatenate([b0, p1, p2, p3], axis=0)
    u1, v1 = shift(first, "y", 1), shift(first, "y", -1)
    fs, gs = [yb], [yb]
    for _ in range(4):
        fs.append(shift(fs[-1], "z", 1))
    for _ in range(3):
        gs.append(shift(gs[-1], "z", -1))
    second = jnp.concatenate([f2, g2, f3, g3, f4], axis=0)
    second, u1, v1 = lax.optimization_barrier((second, u1, v1, *beside))[:3]
    u2, v2 = shift(second, "y", 1), shift(second, "y", -1)
    h1, h2 = (3 * NA + 1) // 2, (5 * NA + 1) // 2
    w11, w12 = shift(u1[:h1], "y", 1), shift(v1[h1:], "y", -1)
    w11, w12, u2, v2 = lax.optimization_barrier((w11, w12, u2, v2))
    w21, w22 = shift(u2[:h2], "y", 1), shift(v2[h2:], "y", -1)
    return [first, second, u1, u2, v1, v2, w11, w12, w21, w22, *fs, *gs[1:]]


EARLY, LATE = 0, 7


def lookup(index, table):
    return sum(jnp.where(index == i, v, 0) for i, v in enumerate(table))


def place_of(ez, ey, j):
    h1, h2 = (3 * NA + 1) // 2, (5 * NA + 1) // 2
    late = ((ez >= 2) & (ez <= 6)).astype(jnp.int32)
    off = lookup(ez, [0, 1, 0, 2, 4, 3, 1, 2]) * NA + j
    half = jnp.where(late == 1, h2, h1)
    upper = off >= half
    piece_a = jnp.where(
        ey == 2,
        6 + 2 * late + upper.astype(jnp.int32),
        lookup(ey, [0, 2, 0, 4]) + late,
    )
    off_a = jnp.where((ey == 2) & upper, off - half, off)
    piece_b = lookup(ez, [10, 11, 12, 13, 14, 17, 16, 15])
    off_b = ey * NB + j - NA
    in_a = j < NA
    return jnp.where(in_a, piece_a, piece_b), jnp.where(in_a, off_a, off_b)


def total_of(mask, axis=-1):
    return jnp.sum(mask, axis=axis, dtype=jnp.int32)


def shards(
    initial_state,
    past_rates,
    stimulus,
    leak_rate,
    local_weight,
    far_weight,
    local_index,
    area_sizes,
    far_area,
    far_offset,
):
    x, z, y, c = (lax.axis_index(n) for n in ("x", "z", "y", "c"))
    first_rate = jax.nn.softplus(initial_state).astype(BF16)

    def section_of(rate):
        parts = [rate] + [shift(rate, "y", g) for g in range(1, NY)]
        return parts + [swap(p) for p in parts]

    section = section_of(first_rate)
    plane0 = gather_plane(past_rates[0], (), section)
    both = lax.all_gather(
        jnp.concatenate([past_rates[1], first_rate], axis=0), ("z", "y"), axis=0, tiled=True
    )

    def mine(table):
        t = table.reshape(NX, NZ, NY, NC, LINKS)
        t = lax.dynamic_index_in_dim(t, z, 1, keepdims=False)
        return lax.dynamic_index_in_dim(t, y, 1, keepdims=False)

    area, offset = mine(far_area), mine(far_offset)
    ids = jnp.arange(area_sizes.shape[0], dtype=jnp.int32)
    starts = jnp.sum(jnp.where(ids[None, :] < ids[:, None], area_sizes[None, :], 0), axis=-1)
    match = area[..., None] == ids
    area_len = jnp.sum(jnp.where(match, area_sizes, 0), axis=-1)
    first = jnp.sum(jnp.where(match, starts, 0), axis=-1)
    block = first * SEC + offset % (area_len * SEC)
    plane = block >> 9
    lids = jnp.arange(LINKS, dtype=jnp.int32)
    earlier = lids[None, :] < lids[:, None]
    rank = total_of((plane[..., :, None] == plane[..., None, :]) & earlier)

    own = lambda t: lax.dynamic_index_in_dim(
        lax.dynamic_index_in_dim(t, x, 0, keepdims=False), c, 0, keepdims=False
    )
    own_plane, own_rank = own(plane), own(rank)
    hop = jnp.arange(NX, dtype=jnp.int32)
    slot = jnp.arange(CAP, dtype=jnp.int32)
    fits = (own_plane == ((x + hop) & 3)[:, None])[:, None, :] & (
        own_rank[None, None, :] == slot[None, :, None]
    )
    pick = after(jnp.sum(jnp.where(fits, lids, 0), axis=-1), plane0[EARLY])
    flat_weight = far_weight.reshape(LINKS, BLK, BLK)
    near = [flat_weight[pick[0]]] + [
        shift(flat_weight[pick[g]], "x", g) for g in range(1, NX)
    ]

    dest_x = jnp.arange(NX, dtype=jnp.int32)[:, None, None]
    dest_c = jnp.arange(NC, dtype=jnp.int32)[None, :, None]
    group = jnp.where(dest_c == c, 0, NX) + ((x - dest_x) & 3) + 0 * plane
    source_z, source_y, source_j = (block >> 6) & 7, (block >> 4) & 3, block & 7
    piece, off = place_of((z - source_z) & 7, (y - source_y) & 3, source_j)
    flat = lambda t: t.reshape(-1)
    works = flat((plane == x) & (((block >> 3) & 1) == c))
    order = flat(group * LINKS + lids)
    before = total_of(works[None, :] & (order[None, :] < order[:, None]))
    value = flat(
        group * ROWS + lids // FAR + (rank << 6) + ((source_z * 64 + source_y * 16 + source_j) << 11)
    )
    spots = jnp.arange(LIST, dtype=jnp.int32)
    links = jnp.sum(
        jnp.where(works[None, :] & (before[None, :] == spots[:, None]), value[None, :], 0), axis=-1
    )
    fetch_order = flat(piece) * 512 + order
    fetch_before = total_of(works[None, :] & (fetch_order[None, :] < fetch_order[:, None]))
    fetch_value = before + (flat(off) << 8)
    fetch = jnp.sum(
        jnp.where(
            works[None, :] & (fetch_before[None, :] == spots[:, None]), fetch_value[None, :], 0
        ),
        axis=-1,
    )
    group_starts = total_of(
        works[None, :] & (flat(group)[None, :] < jnp.arange(GROUPS + 1, dtype=jnp.int32)[:, None])
    )
    piece_starts = total_of(
        works[None, :] & (flat(piece)[None, :] < jnp.arange(PIECES + 1, dtype=jnp.int32)[:, None])
    )
    meta = jnp.concatenate([links, fetch, group_starts, piece_starts])
    weights = pack_weights(meta, near + [swap(w) for w in near])

    col = local_index >> 3
    local_pos = (
        jnp.where((col & 1) == c, 0, 32) + ((y - (col >> 1)) & 3) * 8 + (local_index & 7)
    ).reshape(-1)

    def far_input(parts):
        *kept, other = parts
        other = swap(other).reshape(NX, ROWS, BLK, BLK)
        sums = [kept[g] + other[g] for g in range(NX)]
        return [sums[0]] + [shift(sums[g].astype(BF16), "x", -g) for g in range(1, NX)]

    membrane, rate = initial_state, first_rate
    far = [far_input(partial_sums(meta, weights, plane0, 0)), None, None, None]
    for step in range(STEPS):
        if step == 3:
            plane3[LATE] = after(plane3[LATE], rate)
            far[3] = far_input(partial_sums(meta, weights, plane3, 0))
        membrane, rate = step_of(
            local_pos, membrane, stimulus, leak_rate, local_weight, far[step], section
        )
        if step == 0:
            ready = after(both, rate)
            parts = [
                partial_sums(meta, weights, [ready], offset) for offset in (0, ROWS)
            ]
            far[1], far[2] = far_input(parts[0]), far_input(parts[1])
            plane3 = gather_plane(rate, (parts[0][0], parts[1][0]), ())
        if step < 3:
            section = section_of(rate)
    return membrane


def solution(mesh):
    mesh4 = Mesh(mesh.devices.reshape(NX, NZ, NY, NC), ("x", "z", "y", "c"))
    dev = ("x", "z", "y", "c")
    return jax.shard_map(
        shards,
        mesh=mesh4,
        in_specs=(
            P(dev, None, None),
            P(None, dev, None, None),
            P(dev, None, None),
            P(dev, None),
            P(dev, None, None, None),
            P(dev, None, None, None),
            P(dev, None),
            P(),
            P(),
            P(),
        ),
        out_specs=P(dev, None, None),
        check_vma=False,
    )
```

```python
import jax
import jax.numpy as jnp
from jax import lax
from jax.experimental import pallas as pl
from jax.experimental.pallas import tpu as pltpu
from jax.sharding import Mesh, PartitionSpec as P

STEPS = 4
NX, NZ, NY, NC = 4, 8, 4, 2
ROWS = 8
LOCAL = 12
FAR = 8
LINKS = ROWS * FAR
BLK = 128
SEC = 64
CAP = 32
GROUPS = 2 * NX
LIST = GROUPS * CAP
UNROLL = 8
NA = 5
NB = ROWS - NA
PIECES = 18
F32 = jnp.float32
BF16 = jnp.bfloat16
FETCH = LIST
STARTS = 2 * LIST
BOUNDS = STARTS + GROUPS + 1


def ring(n, shift):
    return [(i, (i + shift) % n) for i in range(n)]


def shift(a, axis, by):
    return lax.ppermute(a, axis, ring({"x": NX, "y": NY, "z": NZ}[axis], by))


def swap(a):
    return lax.ppermute(a, "c", [(0, 1), (1, 0)])


def any_spec():
    return pl.BlockSpec(memory_space=pl.ANY)


def vmem_spec():
    return pl.BlockSpec(memory_space=pltpu.VMEM)


def smem_spec():
    return pl.BlockSpec(memory_space=pltpu.SMEM)


def pack_kernel(meta_ref, *refs):
    pieces, out_ref = refs[:GROUPS], refs[GROUPS]
    held, sem, out_sem = refs[GROUPS + 1 :]
    for q, piece in enumerate(pieces):

        def start(p, carry, piece=piece):
            rank = (meta_ref[p] >> 6) & 31
            pltpu.make_async_copy(piece.at[rank], held.at[p], sem).start()
            return carry

        lax.fori_loop(meta_ref[STARTS + q], meta_ref[STARTS + q + 1], start, 0)

    def wait(p, carry):
        pltpu.make_async_copy(pieces[0].at[0], held.at[0], sem).wait()
        return carry

    count = meta_ref[STARTS + GROUPS]
    lax.fori_loop(0, count, wait, 0)

    def out_copy(i):
        span = pl.ds(pl.multiple_of(i * UNROLL, UNROLL), UNROLL)
        return pltpu.make_async_copy(held.at[span], out_ref.at[span], out_sem)

    def start_out(i, carry):
        out_copy(i).start()
        return carry

    def wait_out(i, carry):
        out_copy(i).wait()
        return carry

    chunks = (count + UNROLL - 1) // UNROLL
    lax.fori_loop(0, chunks, start_out, 0)
    lax.fori_loop(0, chunks, wait_out, 0)


def pack_weights(meta, pieces):
    return pl.pallas_call(
        pack_kernel,
        out_shape=jax.ShapeDtypeStruct((LIST, BLK, BLK), BF16),
        in_specs=[smem_spec()] + [any_spec()] * GROUPS,
        out_specs=any_spec(),
        scratch_shapes=[
            pltpu.VMEM((LIST, BLK, BLK), BF16),
            pltpu.SemaphoreType.DMA,
            pltpu.SemaphoreType.DMA,
        ],
        name="pack_weights",
    )(meta, *pieces)


def make_partial_kernel(n_pieces, offset):
    def kernel(meta_ref, weight_ref, *refs):
        pieces = refs[:n_pieces]
        outs = refs[n_pieces : n_pieces + NX + 1]
        rates, weights, acc, rate_sem, weight_sem, out_sem = refs[n_pieces + NX + 1 :]
        count = meta_ref[STARTS + GROUPS]
        chunks = (count + UNROLL - 1) // UNROLL

        def weight_copy(i):
            span = pl.ds(pl.multiple_of(i * UNROLL, UNROLL), UNROLL)
            return pltpu.make_async_copy(weight_ref.at[span], weights.at[span], weight_sem)

        def start_weight(i, carry):
            weight_copy(i).start()
            return carry

        lax.fori_loop(0, chunks, start_weight, 0)
        if n_pieces == 1:

            def start_rate(p, carry):
                place = (meta_ref[p] >> 11) & 511
                pltpu.make_async_copy(
                    pieces[0].at[place + offset], rates.at[p], rate_sem
                ).start()
                return carry

            lax.fori_loop(0, count, start_rate, 0)
        else:
            for q, piece in enumerate(pieces):

                def start_rate(i, carry, piece=piece):
                    v = meta_ref[FETCH + i]
                    pltpu.make_async_copy(
                        piece.at[(v >> 8) & 63], rates.at[v & 255], rate_sem
                    ).start()
                    return carry

                lax.fori_loop(meta_ref[BOUNDS + q], meta_ref[BOUNDS + q + 1], start_rate, 0)
        acc[...] = jnp.zeros_like(acc)

        def wait_rate(p, carry):
            pltpu.make_async_copy(pieces[0].at[0], rates.at[0], rate_sem).wait()
            return carry

        def wait_weight(i, carry):
            weight_copy(i).wait()
            return carry

        lax.fori_loop(0, count, wait_rate, 0)
        lax.fori_loop(0, chunks, wait_weight, 0)

        def chunk(i, carry):
            prods = []
            for u in range(UNROLL):
                p = i * UNROLL + u
                row = jnp.where(p < count, meta_ref[p] & 63, GROUPS * ROWS)
                prod = lax.dot_general(
                    rates[p], weights[p], (((1,), (1,)), ((), ())), preferred_element_type=F32
                )
                prods.append((row, prod))
            for row, prod in prods:
                acc[row] += prod
            return carry

        lax.fori_loop(0, chunks, chunk, 0)
        copies = [
            pltpu.make_async_copy(acc.at[pl.ds(g * ROWS, ROWS)], outs[g], out_sem.at[g])
            for g in range(NX)
        ] + [
            pltpu.make_async_copy(
                acc.at[pl.ds(NX * ROWS, NX * ROWS)], outs[NX], out_sem.at[NX]
            )
        ]
        for copy in copies:
            copy.start()
        for copy in copies:
            copy.wait()

    return kernel


def partial_sums(meta, weights, pieces, offset):
    return pl.pallas_call(
        make_partial_kernel(len(pieces), offset),
        out_shape=[jax.ShapeDtypeStruct((ROWS, BLK, BLK), F32)] * NX
        + [jax.ShapeDtypeStruct((NX * ROWS, BLK, BLK), F32)],
        in_specs=[smem_spec()] + [any_spec()] * (1 + len(pieces)),
        out_specs=[any_spec()] * (NX + 1),
        scratch_shapes=[
            pltpu.VMEM((LIST, BLK, BLK), BF16),
            pltpu.VMEM((LIST, BLK, BLK), BF16),
            pltpu.VMEM((GROUPS * ROWS + 1, BLK, BLK), F32),
            pltpu.SemaphoreType.DMA,
            pltpu.SemaphoreType.DMA,
            pltpu.SemaphoreType.DMA((NX + 1,)),
        ],
        compiler_params=pltpu.CompilerParams(vmem_limit_bytes=40 * 1024 * 1024),
        name="partial_sums",
    )(meta, weights, *pieces)


def step_kernel(
    pos_ref,
    membrane_ref,
    stimulus_ref,
    leak_ref,
    weight_ref,
    f0_ref,
    f1_ref,
    f2_ref,
    f3_ref,
    *refs,
):
    pieces = refs[:GROUPS]
    out_ref, rate_ref = refs[GROUPS : GROUPS + 2]
    section, sems = refs[GROUPS + 2 :]
    copies = [
        pltpu.make_async_copy(piece, section.at[pl.ds(q * ROWS, ROWS)], sems.at[q])
        for q, piece in enumerate(pieces)
    ]
    for copy in copies:
        copy.start()
    for copy in copies:
        copy.wait()

    def row(i, carry):
        total = f0_ref[i] + f1_ref[i].astype(F32) + f2_ref[i].astype(F32) + f3_ref[i].astype(F32) + stimulus_ref[i].astype(F32)
        for k in range(0, LOCAL, 2):
            left = jnp.concatenate(
                [section[pos_ref[i * LOCAL + k]], section[pos_ref[i * LOCAL + k + 1]]], axis=1
            )
            right = jnp.concatenate([weight_ref[i, k], weight_ref[i, k + 1]], axis=1)
            total += lax.dot_general(
                left, right, (((1,), (1,)), ((), ())), preferred_element_type=F32
            )
        old = membrane_ref[i]
        new = old + leak_ref[pl.ds(i, 1), :] * (total - old)
        out_ref[i] = new
        soft = jnp.maximum(new, 0.0) + jnp.log1p(jnp.exp(-jnp.abs(new)))
        rate_ref[i] = soft.astype(BF16)
        return carry

    lax.fori_loop(0, ROWS, row, 0)


def step_of(pos, membrane, stimulus, leak, weights, far, pieces):
    return pl.pallas_call(
        step_kernel,
        out_shape=[
            jax.ShapeDtypeStruct((ROWS, BLK, BLK), F32),
            jax.ShapeDtypeStruct((ROWS, BLK, BLK), BF16),
        ],
        in_specs=[smem_spec()] + [vmem_spec()] * 8 + [any_spec()] * GROUPS,
        out_specs=[vmem_spec()] * 2,
        scratch_shapes=[
            pltpu.VMEM((SEC, BLK, BLK), BF16),
            pltpu.SemaphoreType.DMA((GROUPS,)),
        ],
        compiler_params=pltpu.CompilerParams(vmem_limit_bytes=24 * 1024 * 1024),
        name="step",
    )(pos, membrane, stimulus, leak, weights, *far, *pieces)


def after(value, *deps):
    return lax.optimization_barrier((value, *deps))[0]


def gather_plane(frame, before, beside):
    a0, b0 = frame[:NA], frame[NA:]
    p1, p3, p2 = shift(b0, "y", 1), shift(b0, "y", -1), shift(b0, "y", 2)
    f1, g1 = shift(a0, "z", 1), shift(a0, "z", -1)
    first = jnp.concatenate([a0, f1, g1], axis=0)
    f2, g2 = shift(f1, "z", 1), shift(g1, "z", -1)
    f3, g3 = shift(f2, "z", 1), shift(g2, "z", -1)
    f4 = shift(f3, "z", 1)
    first, p1, p2, p3 = lax.optimization_barrier((first, p1, p2, p3, *before))[:4]
    yb = jnp.concatenate([b0, p1, p2, p3], axis=0)
    u1, v1 = shift(first, "y", 1), shift(first, "y", -1)
    fs, gs = [yb], [yb]
    for _ in range(4):
        fs.append(shift(fs[-1], "z", 1))
    for _ in range(3):
        gs.append(shift(gs[-1], "z", -1))
    second = jnp.concatenate([f2, g2, f3, g3, f4], axis=0)
    second, u1, v1 = lax.optimization_barrier((second, u1, v1, *beside))[:3]
    u2, v2 = shift(second, "y", 1), shift(second, "y", -1)
    h1, h2 = (3 * NA + 1) // 2, (5 * NA + 1) // 2
    w11, w12 = shift(u1[:h1], "y", 1), shift(v1[h1:], "y", -1)
    w11, w12, u2, v2 = lax.optimization_barrier((w11, w12, u2, v2))
    w21, w22 = shift(u2[:h2], "y", 1), shift(v2[h2:], "y", -1)
    return [first, second, u1, u2, v1, v2, w11, w12, w21, w22, *fs, *gs[1:]]


EARLY, LATE = 0, 7


def lookup(index, table):
    return sum(jnp.where(index == i, v, 0) for i, v in enumerate(table))


def place_of(ez, ey, j):
    h1, h2 = (3 * NA + 1) // 2, (5 * NA + 1) // 2
    late = ((ez >= 2) & (ez <= 6)).astype(jnp.int32)
    off = lookup(ez, [0, 1, 0, 2, 4, 3, 1, 2]) * NA + j
    half = jnp.where(late == 1, h2, h1)
    upper = off >= half
    piece_a = jnp.where(
        ey == 2,
        6 + 2 * late + upper.astype(jnp.int32),
        lookup(ey, [0, 2, 0, 4]) + late,
    )
    off_a = jnp.where((ey == 2) & upper, off - half, off)
    piece_b = lookup(ez, [10, 11, 12, 13, 14, 17, 16, 15])
    off_b = ey * NB + j - NA
    in_a = j < NA
    return jnp.where(in_a, piece_a, piece_b), jnp.where(in_a, off_a, off_b)


def total_of(mask, axis=-1):
    return jnp.sum(mask, axis=axis, dtype=jnp.int32)


def shards(
    initial_state,
    past_rates,
    stimulus,
    leak_rate,
    local_weight,
    far_weight,
    local_index,
    area_sizes,
    far_area,
    far_offset,
):
    x, z, y, c = (lax.axis_index(n) for n in ("x", "z", "y", "c"))
    first_rate = jax.nn.softplus(initial_state).astype(BF16)

    def section_of(rate):
        parts = [rate] + [shift(rate, "y", g) for g in range(1, NY)]
        return parts + [swap(p) for p in parts]

    section = section_of(first_rate)
    plane0 = gather_plane(past_rates[0], (), section)
    both = lax.all_gather(
        jnp.concatenate([past_rates[1], first_rate], axis=0), ("z", "y"), axis=0, tiled=True
    )

    def mine(table):
        t = table.reshape(NX, NZ, NY, NC, LINKS)
        t = lax.dynamic_index_in_dim(t, z, 1, keepdims=False)
        return lax.dynamic_index_in_dim(t, y, 1, keepdims=False)

    area, offset = mine(far_area), mine(far_offset)
    ids = jnp.arange(area_sizes.shape[0], dtype=jnp.int32)
    starts = jnp.sum(jnp.where(ids[None, :] < ids[:, None], area_sizes[None, :], 0), axis=-1)
    match = area[..., None] == ids
    area_len = jnp.sum(jnp.where(match, area_sizes, 0), axis=-1)
    first = jnp.sum(jnp.where(match, starts, 0), axis=-1)
    block = first * SEC + offset % (area_len * SEC)
    plane = block >> 9
    lids = jnp.arange(LINKS, dtype=jnp.int32)
    earlier = lids[None, :] < lids[:, None]
    rank = total_of((plane[..., :, None] == plane[..., None, :]) & earlier)

    own = lambda t: lax.dynamic_index_in_dim(
        lax.dynamic_index_in_dim(t, x, 0, keepdims=False), c, 0, keepdims=False
    )
    own_plane, own_rank = own(plane), own(rank)
    hop = jnp.arange(NX, dtype=jnp.int32)
    slot = jnp.arange(CAP, dtype=jnp.int32)
    fits = (own_plane == ((x + hop) & 3)[:, None])[:, None, :] & (
        own_rank[None, None, :] == slot[None, :, None]
    )
    pick = after(jnp.sum(jnp.where(fits, lids, 0), axis=-1), plane0[EARLY])
    flat_weight = far_weight.reshape(LINKS, BLK, BLK)
    near = [flat_weight[pick[0]]] + [
        shift(flat_weight[pick[g]], "x", g) for g in range(1, NX)
    ]

    dest_x = jnp.arange(NX, dtype=jnp.int32)[:, None, None]
    dest_c = jnp.arange(NC, dtype=jnp.int32)[None, :, None]
    group = jnp.where(dest_c == c, 0, NX) + ((x - dest_x) & 3) + 0 * plane
    source_z, source_y, source_j = (block >> 6) & 7, (block >> 4) & 3, block & 7
    piece, off = place_of((z - source_z) & 7, (y - source_y) & 3, source_j)
    flat = lambda t: t.reshape(-1)
    works = flat((plane == x) & (((block >> 3) & 1) == c))
    order = flat(group * LINKS + lids)
    before = total_of(works[None, :] & (order[None, :] < order[:, None]))
    value = flat(
        group * ROWS + lids // FAR + (rank << 6) + ((source_z * 64 + source_y * 16 + source_j) << 11)
    )
    spots = jnp.arange(LIST, dtype=jnp.int32)
    links = jnp.sum(
        jnp.where(works[None, :] & (before[None, :] == spots[:, None]), value[None, :], 0), axis=-1
    )
    fetch_order = flat(piece) * 512 + order
    fetch_before = total_of(works[None, :] & (fetch_order[None, :] < fetch_order[:, None]))
    fetch_value = before + (flat(off) << 8)
    fetch = jnp.sum(
        jnp.where(
            works[None, :] & (fetch_before[None, :] == spots[:, None]), fetch_value[None, :], 0
        ),
        axis=-1,
    )
    group_starts = total_of(
        works[None, :] & (flat(group)[None, :] < jnp.arange(GROUPS + 1, dtype=jnp.int32)[:, None])
    )
    piece_starts = total_of(
        works[None, :] & (flat(piece)[None, :] < jnp.arange(PIECES + 1, dtype=jnp.int32)[:, None])
    )
    meta = jnp.concatenate([links, fetch, group_starts, piece_starts])
    weights = pack_weights(meta, near + [swap(w) for w in near])

    col = local_index >> 3
    local_pos = (
        jnp.where((col & 1) == c, 0, 32) + ((y - (col >> 1)) & 3) * 8 + (local_index & 7)
    ).reshape(-1)

    def far_input(parts):
        *kept, other = parts
        other = swap(other).reshape(NX, ROWS, BLK, BLK)
        sums = [kept[g] + other[g] for g in range(NX)]
        return [sums[0]] + [shift(sums[g].astype(BF16), "x", -g) for g in range(1, NX)]

    membrane, rate = initial_state, first_rate
    far = [far_input(partial_sums(meta, weights, plane0, 0)), None, None, None]
    for step in range(STEPS):
        if step == 2:
            plane3[LATE] = after(plane3[LATE], rate)
            far[3] = far_input(partial_sums(meta, weights, plane3, 0))
            membrane = after(membrane, far[3][0])
        membrane, rate = step_of(
            local_pos, membrane, stimulus, leak_rate, local_weight, far[step], section
        )
        if step == 0:
            ready = after(both, rate)
            parts = [
                partial_sums(meta, weights, [ready], offset) for offset in (0, ROWS)
            ]
            far[1], far[2] = far_input(parts[0]), far_input(parts[1])
            plane3 = gather_plane(rate, (parts[0][0], parts[1][0]), ())
        if step < 3:
            section = section_of(rate)
    return membrane


def solution(mesh):
    mesh4 = Mesh(mesh.devices.reshape(NX, NZ, NY, NC), ("x", "z", "y", "c"))
    dev = ("x", "z", "y", "c")
    return jax.shard_map(
        shards,
        mesh=mesh4,
        in_specs=(
            P(dev, None, None),
            P(None, dev, None, None),
            P(dev, None, None),
            P(dev, None),
            P(dev, None, None, None),
            P(dev, None, None, None),
            P(dev, None),
            P(),
            P(),
            P(),
        ),
        out_specs=P(dev, None, None),
        check_vma=False,
    )
```
